512 devices in a mesh: fsdp: 128 (over y, z_lo, x), dp: 4 (over z_hi, core).
Axes of the slice: x: 4, y: 8, z: 8 (z_hi: 2, z_lo: 4; z = z_hi * 4 + z_lo), core: 2. Of those that a mesh axis runs over, the one named last changes fastest.
Arguments:
- candidate_layer_inputs: bfloat16 [2048, 32, 8192], P(('dp', 'fsdp')), parts along dimension 0, may hold values from -8 to 8
- candidate_loss_cotangent: bfloat16 [2048, 32, 1024], P(('dp', 'fsdp')), parts along dimension 0, may hold values from -8 to 8
- candidate_live_lengths: int32 [2048], P(('dp', 'fsdp')), parts along dimension 0, may hold values from 4 to 32, as said below
- probe_layer_inputs: bfloat16 [2048, 32, 8192], P(('dp', 'fsdp')), parts along dimension 0, may hold values from -8 to 8
- probe_loss_cotangent: bfloat16 [2048, 32, 1024], P(('dp', 'fsdp')), parts along dimension 0, may hold values from -8 to 8
- probe_live_lengths: int32 [2048], P(('dp', 'fsdp')), parts along dimension 0, may hold values from 4 to 32, as said below
- adapter_down_matrix: bfloat16 [8192, 128], P('fsdp'), may hold values from -0.0625 to 0.0625
- adapter_up_matrix: bfloat16 [1024, 128], P('fsdp'), may hold values from -0.5 to 0.5
- input_side_sketch: bfloat16 [8192, 256], P('fsdp'), may hold values from -0.0625 to 0.0625
- output_side_sketch: bfloat16 [1024, 256], P('fsdp'), may hold values from -0.1875 to 0.1875
- rank_sketch_down: bfloat16 [128, 16], replicated, may hold values from -0.5 to 0.5
- rank_sketch_up: bfloat16 [128, 16], replicated, may hold values from -0.5 to 0.5
Outputs:
- scores: float32 [2048, 512], P(('dp', 'fsdp')), parts along dimension 0
- features: bfloat16 [2048, 8192], P(('dp', 'fsdp')), parts along dimension 0
The draws below stay inside these ranges and needn't reach their ends.
There are 4 independent parts, one for each index of `dp`. The reference program is written for one: setup_inputs(seed, part) draws one part's arguments, and reference() takes and returns one part's arrays. A program takes and returns all parts, laid end to end along the dimension named above; an argument that names none is the same for every part. Nothing has to cross between parts.
Inputs may be any that keep to these rules, and one draw needn't show every extreme that they name: `candidate_live_lengths`: the live positions of an example are its first that many; some example has exactly 32 live positions and some exactly 4. `probe_live_lengths`: the live positions of an example are its first that many; some example has exactly 32 live positions and some exactly 4.
All inputs are finite; a program needn't handle non-finite values.
Results may differ from the reference program's by a relative error of at most 0.0056.
Values may be sent and summed in bfloat16 or wider, within the bound.
A program may use at most 64 MiB of HBM per device.

```python
import jax
import jax.numpy as jnp
from jax import lax

MODEL_DIM = 8192
VALUE_WIDTH = 1024
ADAPTER_RANK = 128
KP = 256
KS = 16
SEQ = 32
TRAIN = 512
PROBES = 512


def activation_draw(key, salt, shared_salt, count, seq_len, model_width):
    shared_key = jax.random.fold_in(key, shared_salt)
    noise_key = jax.random.fold_in(key, salt)
    shared_row = 0.5 * jax.random.normal(shared_key, (model_width,), jnp.float32)
    noise = jax.random.normal(noise_key, (count, seq_len, model_width), jnp.float32)
    values = shared_row + noise
    return jnp.clip(values, -8.0, 8.0)


def length_draw(key, salt, count):
    base = jax.random.randint(jax.random.fold_in(key, salt), (count,), SEQ // 8, SEQ + 1)
    order = jax.random.permutation(jax.random.fold_in(key, salt + 1), count)
    base = base.at[order[0]].set(SEQ)
    base = base.at[order[1]].set(SEQ // 8)
    return base.astype(jnp.int32)


def draw_candidate_layer_inputs(key, part):
    return activation_draw(key, 11, 501, TRAIN, SEQ, MODEL_DIM).astype(jnp.bfloat16)


def draw_probe_layer_inputs(key, part):
    return activation_draw(key, 21, 501, PROBES, SEQ, MODEL_DIM).astype(jnp.bfloat16)


def draw_candidate_loss_cotangent(key, part):
    return activation_draw(key, 31, 502, TRAIN, SEQ, VALUE_WIDTH).astype(jnp.bfloat16)


def draw_probe_loss_cotangent(key, part):
    return activation_draw(key, 41, 502, PROBES, SEQ, VALUE_WIDTH).astype(jnp.bfloat16)


def draw_candidate_live_lengths(key, part):
    return length_draw(key, 61, TRAIN)


def draw_probe_live_lengths(key, part):
    return length_draw(key, 71, PROBES)


def level_of(key, extent, shards, smallest, high):
    def one(position, blocks):
        steps = jax.random.uniform(jax.random.fold_in(jax.random.fold_in(key, 6), position), (blocks,), jnp.float32, smallest / len(shards), high / len(shards))
        return jnp.repeat(jnp.exp(steps), extent[position] // blocks).reshape((-1,) + (1,) * (len(extent) - position - 1))

    gain = one(*shards[0])
    for cut in shards[1:]:
        gain = gain * one(*cut)
    return gain


def scatter_about(rng, shape, width, bound, shards=(), kind=jnp.bfloat16):
    gain = level_of(rng, shape, shards, -0.22, 0.18) if shards else 1.0
    values = jax.random.normal(rng, shape, jnp.float32) * width * gain
    return jnp.minimum(jnp.maximum(values, -bound), bound).astype(kind)


def setup_inputs(seed: int = 0, part: int = 0) -> dict:
    seeds = jax.random.split(jax.random.key(seed), 13)
    part_splits = jax.random.split(jax.random.fold_in(seeds[12], part), 13)
    candidate_layer_inputs = draw_candidate_layer_inputs(jax.random.fold_in(jax.random.fold_in(seeds[12], part), 71), part)
    candidate_loss_cotangent = draw_candidate_loss_cotangent(jax.random.fold_in(jax.random.fold_in(seeds[12], part), 71), part)
    candidate_live_lengths = draw_candidate_live_lengths(jax.random.fold_in(jax.random.fold_in(seeds[12], part), 71), part)
    probe_layer_inputs = draw_probe_layer_inputs(jax.random.fold_in(jax.random.fold_in(seeds[12], part), 71), part)
    probe_loss_cotangent = draw_probe_loss_cotangent(jax.random.fold_in(jax.random.fold_in(seeds[12], part), 71), part)
    probe_live_lengths = draw_probe_live_lengths(jax.random.fold_in(jax.random.fold_in(seeds[12], part), 71), part)
    adapter_down_matrix = scatter_about(seeds[6], (MODEL_DIM, ADAPTER_RANK), MODEL_DIM ** -0.5, 0.0625, ((0, 128),))
    adapter_up_matrix = scatter_about(seeds[7], (VALUE_WIDTH, ADAPTER_RANK), ADAPTER_RANK ** -0.5, 0.5, ((0, 128),))
    input_side_sketch = scatter_about(seeds[8], (MODEL_DIM, KP), MODEL_DIM ** -0.5, 0.0625, ((0, 128),))
    output_side_sketch = scatter_about(seeds[9], (VALUE_WIDTH, KP), VALUE_WIDTH ** -0.5, 0.1875, ((0, 128),))
    rank_sketch_down = scatter_about(seeds[10], (ADAPTER_RANK, KS), ADAPTER_RANK ** -0.5, 0.5)
    rank_sketch_up = scatter_about(seeds[11], (ADAPTER_RANK, KS), ADAPTER_RANK ** -0.5, 0.5)
    return {"candidate_layer_inputs": candidate_layer_inputs, "candidate_loss_cotangent": candidate_loss_cotangent, "candidate_live_lengths": candidate_live_lengths, "probe_layer_inputs": probe_layer_inputs, "probe_loss_cotangent": probe_loss_cotangent, "probe_live_lengths": probe_live_lengths, "adapter_down_matrix": adapter_down_matrix, "adapter_up_matrix": adapter_up_matrix, "input_side_sketch": input_side_sketch, "output_side_sketch": output_side_sketch, "rank_sketch_down": rank_sketch_down, "rank_sketch_up": rank_sketch_up}


eps_mean = 1e-06

def live_cotangent(loss_cotangent, example_lengths):
    positions = lax.broadcasted_iota(jnp.int32, loss_cotangent.shape[:2], 1)
    live_mask = (positions < example_lengths[:, None]).astype(loss_cotangent.dtype)
    return loss_cotangent * live_mask[:, :, None]

def compute_sketch_features(down_total_acc, inward_total_acc, loss_cotangent, example_lengths, adapter_up_matrix, output_side_sketch, rank_sketch_down, rank_sketch_up):
    examples = loss_cotangent.shape[0]
    seq_len = loss_cotangent.shape[1]
    kv_width = loss_cotangent.shape[2]
    masked_values = live_cotangent(loss_cotangent, example_lengths).reshape(examples * seq_len, kv_width)
    gradient_rowset = jnp.dot(masked_values, adapter_up_matrix, preferred_element_type=jnp.float32).astype(jnp.bfloat16)
    outward = jnp.dot(masked_values, output_side_sketch, preferred_element_type=jnp.float32).astype(jnp.bfloat16)
    down_round = down_total_acc.astype(jnp.bfloat16)
    inward_round = inward_total_acc.astype(jnp.bfloat16)
    left_small = jnp.dot(gradient_rowset, rank_sketch_down, preferred_element_type=jnp.float32).astype(jnp.bfloat16)
    right_small = jnp.dot(down_round, rank_sketch_up, preferred_element_type=jnp.float32).astype(jnp.bfloat16)
    small_cols = rank_sketch_down.shape[1]
    large_cols = inward_round.shape[1]
    grad_left = jnp.einsum('esk,esp->ekp', left_small.reshape(examples, seq_len, small_cols).astype(jnp.float32), inward_round.reshape(examples, seq_len, large_cols).astype(jnp.float32), precision=lax.Precision.HIGHEST)
    grad_right = jnp.einsum('esk,esp->ekp', right_small.reshape(examples, seq_len, small_cols).astype(jnp.float32), outward.reshape(examples, seq_len, large_cols).astype(jnp.float32), precision=lax.Precision.HIGHEST)
    joined = jnp.concatenate([grad_left, grad_right], axis=1).reshape(examples, 2 * small_cols * large_cols)
    inv_rms = lax.rsqrt(lax.optimization_barrier(jnp.mean(joined * joined, axis=1, keepdims=True)) + eps_mean)
    return (joined * inv_rms).astype(jnp.bfloat16)

def reference(candidate_layer_inputs, candidate_loss_cotangent, candidate_live_lengths, probe_layer_inputs, probe_loss_cotangent, probe_live_lengths, adapter_down_matrix, adapter_up_matrix, input_side_sketch, output_side_sketch, rank_sketch_down, rank_sketch_up):

    def one_side(inputs, loss_cotangent, example_lengths):
        model_width = inputs.shape[2]
        flattened_rowset = inputs.reshape(-1, model_width)
        down_total_acc = jnp.dot(flattened_rowset, adapter_down_matrix, preferred_element_type=jnp.float32)
        inward_total_acc = jnp.dot(flattened_rowset, input_side_sketch, preferred_element_type=jnp.float32)
        return compute_sketch_features(down_total_acc, inward_total_acc, loss_cotangent, example_lengths, adapter_up_matrix, output_side_sketch, rank_sketch_down, rank_sketch_up)
    features = one_side(candidate_layer_inputs, candidate_loss_cotangent, candidate_live_lengths)
    probe_features = one_side(probe_layer_inputs, probe_loss_cotangent, probe_live_lengths)
    scores = jnp.dot(features, probe_features.T, preferred_element_type=jnp.float32) / features.shape[1]
    return (scores, features)
```

```python
import jax
import jax.numpy as jnp
from jax import lax
from jax.experimental import pallas as pl
from jax.experimental.pallas import tpu as pltpu
from jax.sharding import Mesh
from jax.sharding import PartitionSpec as P

AXES = ("y", "zl", "x", "zh", "core")
FSDP = ("y", "zl", "x")
DP_FSDP = ("zh", "core", "y", "zl", "x")
NY, NZ, NX = 8, 4, 4
SEQ = 32
EPS = 1e-06
BF, F32 = jnp.bfloat16, jnp.float32

ROWS = {"Y": (0, 32), "X": (32, 32), "Z": (64, 16)}
ORDER = {"Y": "xzy", "X": "yzx", "Z": "yxz"}
N_SEMS = 96
PARTNERS = 16

SCHEDULE = (
    [(q, s) for s in range(4) for q in "YXZ"]
    + [("X", 4), ("Z", 4), ("Y", 4), ("X", 5), ("Z", 5), ("X", 6), ("Z", 6), ("Y", 5), ("Y", 6)]
    + [("Z", 7), ("X", 7), ("Y", 7)]
    + [("Z", 8), ("X", 8), ("Y", 8)]
)


def nt(a, b):
    return lax.dot_general(a, b, (((1,), (1,)), ((), ())), preferred_element_type=F32)


def nn(a, b):
    return jnp.dot(a, b, preferred_element_type=F32)


def iota(shape, dim):
    return lax.broadcasted_iota(jnp.int32, shape, dim)


def one_hot_rows(rows, cols, per):
    return (iota((rows, cols), 0) // per == iota((rows, cols), 1)).astype(F32).astype(BF)


def kernel(
    xc, ct_c, len_c, xp, ct_p, len_p, down, up, win, wout, rk_down, rk_up,
    scores, feats,
    gath, xs, cot, masked, spread, taken, fblk, pblk, tsum, tgot, vsum, vgot,
    ld_sem, send_sem, recv_sem,
):
    y, zl, x = (lax.axis_index(a) for a in FSDP)
    zh, core = lax.axis_index("zh"), lax.axis_index("core")
    zz = zh * NZ + zl

    def at(dy=0, dx=0, dz=0, z_in=None, other=False):
        if z_in is None:
            full = lax.rem(zz + dz + 8, 8)
            tz, th = lax.rem(full, NZ), full // NZ
        else:
            tz, th = z_in, zh
        return (
            lax.rem(y + dy + NY, NY),
            tz,
            lax.rem(x + dx + NX, NX),
            th,
            1 - core if other else core,
        )

    loads = [
        pltpu.make_async_copy(src, dst, ld_sem.at[k])
        for k, (src, dst) in enumerate(
            (
                (ct_c, cot.at[pl.ds(0, 128)]),
                (ct_p, cot.at[pl.ds(128, 128)]),
                (xc, xs.at[pl.ds(0, 128)]),
                (xp, xs.at[pl.ds(128, 128)]),
            )
        )
    ]
    for c in loads:
        c.start()

    barrier = pltpu.get_barrier_semaphore()
    partners = [at(dy=d) for d in range(1, NY)] + [at(dx=d) for d in range(1, NX)]
    partners += [at(z_in=lax.rem(zl + d, NZ)) for d in range(1, NZ)]
    partners += [at(dz=1), at(dz=-1), at(other=True)]
    for dev in partners:
        pl.semaphore_signal(barrier, inc=1, device_id=dev, device_id_type=pl.DeviceIdType.MESH)

    ru = nt(one_hot_rows(16, 16, 1), rk_up[...])
    top, bottom = ru[0:8], ru[8:16]
    odd = lax.rem(x, 2) == 1
    left = jnp.where(odd, bottom, top)
    right = jnp.where(odd, top, bottom)
    dn = down[...]
    zero = jnp.zeros_like(dn)
    wide = jnp.concatenate(
        [jnp.concatenate([dn, zero], axis=1), jnp.concatenate([zero, dn], axis=1)], axis=0
    )
    fold = nt(jnp.concatenate([left, right], axis=1).astype(BF), wide)
    aux_1 = jnp.concatenate([fold, up[...].astype(F32)], axis=0)
    wo = wout[...].astype(F32)
    aux_0 = jnp.concatenate([wo[:, :128], wo[:, 128:]], axis=0)
    first = core == 0
    gath[core, y, zl, x, 0:64, :] = jnp.where(
        first, win[:, :128].astype(F32), win[:, 128:].astype(F32)
    ).astype(BF)
    gath[core, y, zl, x, 64:80, :] = jnp.where(first, aux_0, aux_1).astype(BF)

    pl.semaphore_wait(barrier, PARTNERS)

    used = [0]
    begun = []

    def send(src, dst, dev):
        k = used[0]
        used[0] += 1
        c = pltpu.make_async_remote_copy(
            src_ref=src,
            dst_ref=dst,
            send_sem=send_sem.at[k],
            recv_sem=recv_sem.at[k],
            device_id=dev,
            device_id_type=pl.DeviceIdType.MESH,
        )
        c.start()
        begun.append(c)
        return c

    size = {"x": NX, "y": NY, "z": NZ}
    here = {"x": x, "y": y, "z": zl}

    def block(q, phase, p, half):
        r0, n = ROWS[q]
        order = ORDER[q]
        idx = {}
        for a in order[:phase]:
            idx[a] = slice(None)
        for a in order[phase:]:
            idx[a] = here[a]
        idx[order[phase]] = p
        if half is not None:
            if phase == 0:
                if n >= 32:
                    r0, n = r0 + half * (n // 2), n // 2
                elif half == 1:
                    return None
            else:
                a = order[0]
                idx[a] = pl.ds(half * (size[a] // 2), size[a] // 2)
        return gath.at[core, idx["y"], idx["z"], idx["x"], pl.ds(r0, n), :]

    def steps(q):
        out = []
        for phase, a in enumerate(ORDER[q]):
            for t in range(1, size[a] // 2 + 1):
                out.append((phase, a, t))
        return out

    chain = {q: steps(q) for q in "YXZ"}
    flying = {q: [] for q in "YXZ"}
    swaps = []

    def swap(q, p):
        b = block(q, 2, p, None)
        swaps.append(send(b, b, at(other=True)))

    def advance(q, s):
        for c in flying[q]:
            c.wait_recv()
        flying[q] = []
        if s > 0:
            phase, a, t = chain[q][s - 1]
            if phase == 2:
                n = size[a]
                swap(q, lax.rem(here[a] - t + n, n))
                if t < n // 2:
                    swap(q, lax.rem(here[a] + t, n))
        if s < 8:
            phase, a, t = chain[q][s]
            n = size[a]
            if phase == 2 and t == 1:
                swap(q, here[a])
            last = t == n // 2
            for sign in (1, -1):
                p = lax.rem(here[a] - sign * (t - 1) + n, n)
                b = block(q, phase, p, (0 if sign == 1 else 1) if last else None)
                if b is not None:
                    flying[q].append(send(b, b, at(**{"d" + a: sign})))

    def mask_rows():
        loads[0].wait()
        loads[1].wait()
        pos = iota((SEQ, 1024), 0)
        for e in range(8):
            live = (len_c if e < 4 else len_p)[e % 4]
            rows = cot[e * SEQ : (e + 1) * SEQ, :].astype(F32)
            masked[e * SEQ : (e + 1) * SEQ, :] = jnp.where(pos < live, rows, 0.0).astype(BF)

    for k, (q, s) in enumerate(SCHEDULE):
        advance(q, s)
        if k == 2:
            mask_rows()
    loads[2].wait()
    loads[3].wait()
    for c in swaps:
        c.wait_recv()

    low = iota((8, 8, 128), 2) < 64

    def plane(k, acc):
        inward, right_sum, grad, outward = acc
        lanes = pl.ds(pl.multiple_of(k * 1024, 1024), 1024)
        xk = xs[:, lanes]
        w = jnp.concatenate(
            [gath[h, k, :, :, 0:64, :].reshape(1024, 128) for h in range(2)], axis=1
        )
        inward = inward + nn(xk, w)
        a0 = gath[0, k, :, :, 64:80, :].reshape(16, 16, 128).astype(F32)
        a1 = gath[1, k, :, :, 64:80, :].reshape(16, 16, 128).astype(F32)
        wo_k = jnp.concatenate(
            [a0[:, 0:8].reshape(128, 128), a0[:, 8:16].reshape(128, 128)], axis=1
        ).astype(BF)
        up_k = a1[:, 8:16].reshape(128, 128).astype(BF)
        pairs = a1[:, 0:8].reshape(8, 2, 8, 128)
        te, to = pairs[:, 0], pairs[:, 1]
        t8 = jnp.where(low, te, to)
        b8 = pltpu.roll(jnp.where(low, to, te), 64, 2)
        fold_t = jnp.concatenate(
            [jnp.concatenate([t8[m], b8[m]], axis=0) for m in range(8)], axis=1
        ).astype(BF)
        right_sum = right_sum + nt(xk, fold_t)
        mk = masked[:, pl.ds(pl.multiple_of(k * 128, 128), 128)]
        grad = grad + nn(mk, up_k)
        outward = outward + nn(mk, wo_k)
        return inward, right_sum, grad, outward

    zeros = lambda n: jnp.zeros((256, n), F32)
    inward, right_sum, grad, outward = lax.fori_loop(
        0, NY, plane, (zeros(256), zeros(16), zeros(128), zeros(256))
    )

    own = lax.rem(iota((128, 256), 0), 8) == iota((128, 256), 1) // SEQ
    spread_k = one_hot_rows(128, 16, 8)
    rd = nt(spread_k, rk_down[...]).astype(BF)
    left_t = jnp.where(own, nt(rd, grad.astype(BF)), 0.0).astype(BF)
    right_t = jnp.where(own, nt(spread_k, right_sum.astype(BF)), 0.0).astype(BF)
    gl = nn(left_t, inward.astype(BF))
    gr = nn(right_t, outward.astype(BF))
    joined = jnp.concatenate(
        [g[8 * k : 8 * k + 8] for g in (gl, gr) for k in range(16)], axis=1
    )
    inv = lax.rsqrt(jnp.sum(joined * joined, axis=1, keepdims=True) / 8192.0 + EPS)
    normed = joined * inv
    feats[...] = normed.astype(BF)

    for b in range(NY):
        part = normed[:, 1024 * b : 1024 * b + 1024]
        spread[b] = jnp.concatenate([part[:, :512], part[:, 512:]], axis=0).astype(BF)
    taken[y] = spread[y]
    moved = [
        send(spread.at[lax.rem(y + d, NY)], taken.at[y], at(dy=d)) for d in (4, 3, 5, 2, 6, 1, 7)
    ]
    for c in moved:
        c.wait_recv()
    upper = iota((8, 1024), 0) < 4
    f_rows, p_rows = [], []
    for m in range(4):
        a, b = (
            jnp.concatenate([v[0:8], v[8:16]], axis=1)
            for v in (taken[2 * m].astype(F32), taken[2 * m + 1].astype(F32))
        )
        f_rows.append(jnp.where(upper, a, pltpu.roll(b, 4, 0)))
        p_rows.append(jnp.where(upper, pltpu.roll(a, 4, 0), b))
    fblk[zl] = jnp.concatenate(f_rows, axis=0).astype(BF)
    pblk[x] = jnp.concatenate(p_rows, axis=0).astype(BF)
    moved = []
    for d in range(1, NZ):
        moved.append(send(fblk.at[zl], fblk.at[zl], at(z_in=lax.rem(zl + d, NZ))))
    for d in (2, 1, 3):
        moved.append(send(pblk.at[x], pblk.at[x], at(dx=d)))
    for c in moved:
        c.wait_recv()
    prod = nt(fblk[...].reshape(128, 1024), pblk[...].reshape(128, 1024))

    upper = iota((8, 128), 0) < 4
    tile = lambda zq, m: prod[zq * 32 + m * 8 : zq * 32 + m * 8 + 8]
    for m in range(4):
        for h in range(2):
            a, b = tile(2 * h, m), tile(2 * h + 1, m)
            tsum[2 * m, 8 * h : 8 * h + 8] = jnp.where(upper, a, pltpu.roll(b, 4, 0))
            tsum[2 * m + 1, 8 * h : 8 * h + 8] = jnp.where(upper, pltpu.roll(a, 4, 0), b)
    tgot[y] = tsum[y]
    moved = [
        send(tsum.at[lax.rem(y + d, NY)], tgot.at[y], at(dy=d)) for d in (4, 3, 5, 2, 6, 1, 7)
    ]
    for c in moved:
        c.wait_recv()
    total = tgot[0]
    for k in range(1, NY):
        total = total + tgot[k]
    vsum[0] = total[0:8]
    vsum[1] = total[8:16]
    vgot[zl] = vsum[zl // 2]
    moved = []
    for d in range(1, NZ):
        tz = lax.rem(zl + d, NZ)
        moved.append(send(vsum.at[tz // 2], vgot.at[zl], at(z_in=tz)))

    src, col = iota((512, 512), 0), iota((512, 512), 1)
    want = ((col // 16) % 4) * 128 + ((col // 4) % 4) * 32 + (col // 64) * 4 + col % 4
    perm = (src == want).astype(F32).astype(BF)
    for c in moved:
        c.wait_recv()
    odd_z = lax.rem(zl, 2) == 1
    flat = jnp.concatenate(
        [jnp.where(odd_z, pltpu.roll(vgot[k], 4, 0), vgot[k]) for k in range(NZ)], axis=1
    )
    p1 = flat.astype(BF)
    rest = flat - p1.astype(F32)
    p2 = rest.astype(BF)
    p3 = (rest - p2.astype(F32)).astype(BF)
    out = nn(p1, perm) + nn(p2, perm) + nn(p3, perm)
    scores[...] = out * (1.0 / 8192.0)

    for c in begun:
        c.wait_send()


def body(xc, ct_c, len_c, xp, ct_p, len_p, down, up, win, wout, rk_down, rk_up):
    width, values = xc.shape[2], ct_c.shape[2]
    anyspace = pl.BlockSpec(memory_space=pl.ANY)
    vmem = pl.BlockSpec(memory_space=pltpu.VMEM)
    smem = pl.BlockSpec(memory_space=pltpu.SMEM)
    scores, feats = pl.pallas_call(
        kernel,
        out_shape=(
            jax.ShapeDtypeStruct((8, 512), F32),
            jax.ShapeDtypeStruct((8, 8192), BF),
        ),
        in_specs=[anyspace, anyspace, smem, anyspace, anyspace, smem] + [vmem] * 6,
        out_specs=(vmem, vmem),
        scratch_shapes=[
            pltpu.VMEM((2, NY, NZ, NX, 80, 128), BF),
            pltpu.VMEM((256, 8192), BF),
            pltpu.VMEM((256, 1024), BF),
            pltpu.VMEM((256, 1024), BF),
            pltpu.VMEM((NY, 16, 512), BF),
            pltpu.VMEM((NY, 16, 512), BF),
            pltpu.VMEM((NZ, 32, 1024), BF),
            pltpu.VMEM((NX, 32, 1024), BF),
            pltpu.VMEM((NY, 16, 128), F32),
            pltpu.VMEM((NY, 16, 128), F32),
            pltpu.VMEM((2, 8, 128), F32),
            pltpu.VMEM((NZ, 8, 128), F32),
            pltpu.SemaphoreType.DMA((4,)),
            pltpu.SemaphoreType.DMA((N_SEMS,)),
            pltpu.SemaphoreType.DMA((N_SEMS,)),
        ],
        compiler_params=pltpu.CompilerParams(
            collective_id=0, has_side_effects=True, vmem_limit_bytes=48 * 1024 * 1024
        ),
        name="lora_scores",
    )(
        xc.reshape(-1, width), ct_c.reshape(-1, values), len_c,
        xp.reshape(-1, width), ct_p.reshape(-1, values), len_p,
        down, up, win, wout, rk_down, rk_up,
    )
    return scores[:4], feats[:4]


def solution(mesh):
    split = Mesh(mesh.devices.reshape(NY, NZ, NX, 2, 2), AXES)
    rows = P(FSDP, None)
    whole = P(DP_FSDP, None, None)
    return jax.shard_map(
        body,
        mesh=split,
        in_specs=(
            whole, whole, P(DP_FSDP), whole, whole, P(DP_FSDP), rows, rows, rows, rows, P(), P(),
        ),
        out_specs=(P(DP_FSDP, None), P(DP_FSDP, None)),
        check_vma=False,
    )
```

```python
import jax
import jax.numpy as jnp
from jax import lax
from jax.experimental import pallas as pl
from jax.experimental.pallas import tpu as pltpu
from jax.sharding import Mesh
from jax.sharding import PartitionSpec as P

AXES = ("y", "zl", "x", "zh", "core")
FSDP = ("y", "zl", "x")
DP_FSDP = ("zh", "core", "y", "zl", "x")
NY, NZ, NX = 8, 4, 4
SEQ = 32
EPS = 1e-06
BF, F32 = jnp.bfloat16, jnp.float32

N_SEMS = 192


def nt(a, b):
    return lax.dot_general(a, b, (((1,), (1,)), ((), ())), preferred_element_type=F32)


def nn(a, b):
    return jnp.dot(a, b, preferred_element_type=F32)


def iota(shape, dim):
    return lax.broadcasted_iota(jnp.int32, shape, dim)


def one_hot_rows(rows, cols, per):
    return (iota((rows, cols), 0) // per == iota((rows, cols), 1)).astype(F32).astype(BF)


def kernel(
    xc, ct_c, len_ch, xp, ct_p, len_ph, down_h, up_h, win_h, wout_h, rk_down_h, rk_up_h,
    scores, feats,
    len_c, len_p, down, up, wout, rk_down, rk_up,
    gath, xs, cot, masked, spread, taken, fblk, pblk, tsum, tgot, vsum, vgot,
    ld_sem, send_sem, recv_sem,
):
    y, zl, x = (lax.axis_index(a) for a in FSDP)
    zh, core = lax.axis_index("zh"), lax.axis_index("core")
    zz = zh * NZ + zl

    def at(dy=0, dx=0, dz=0, z_in=None, other=False):
        if z_in is None:
            full = lax.rem(zz + dz + 8, 8)
            tz, th = lax.rem(full, NZ), full // NZ
        else:
            tz, th = z_in, zh
        return (
            lax.rem(y + dy + NY, NY),
            tz,
            lax.rem(x + dx + NX, NX),
            th,
            1 - core if other else core,
        )

    loads = [
        pltpu.make_async_copy(src, dst, ld_sem.at[k])
        for k, (src, dst) in enumerate(
            (
                (rk_up_h, rk_up),
                (down_h, down),
                (up_h, up),
                (win_h.at[:, pl.ds(pl.multiple_of(core * 128, 128), 128)], gath.at[core, y, zl, x, pl.ds(0, 64)]),
                (wout_h, wout),
                (rk_down_h, rk_down),
                (len_ch, len_c),
                (len_ph, len_p),
                (ct_c, cot.at[pl.ds(0, 128)]),
                (ct_p, cot.at[pl.ds(128, 128)]),
                (xc, xs.at[pl.ds(0, 128)]),
                (xp, xs.at[pl.ds(128, 128)]),
            )
        )
    ]
    for c in loads:
        c.start()

    barrier = pltpu.get_barrier_semaphore()
    partners = [at(dy=d) for d in range(1, NY)] + [at(dx=d) for d in range(1, NX)]
    partners += [at(z_in=lax.rem(zl + d, NZ)) for d in range(1, NZ)]
    partners += [at(dz=d) for d in (1, -1, 2, -2)] + [at(other=True)]
    for dev in partners:
        pl.semaphore_signal(barrier, inc=1, device_id=dev, device_id_type=pl.DeviceIdType.MESH)

    for c in loads[:8]:
        c.wait()

    ru = rk_up[...].astype(F32)
    top, bottom = ru[0:8], ru[8:16]
    odd = lax.rem(x, 2) == 1
    left = jnp.where(odd, bottom, top)
    right = jnp.where(odd, top, bottom)
    dn = down[...]
    zero = jnp.zeros_like(dn)
    wide = jnp.concatenate(
        [jnp.concatenate([dn, zero], axis=1), jnp.concatenate([zero, dn], axis=1)], axis=0
    )
    fold = nt(jnp.concatenate([left, right], axis=1).astype(BF), wide)
    aux_1 = jnp.concatenate([fold, up[...].astype(F32)], axis=0)
    wo = wout[...].astype(F32)
    aux_0 = jnp.concatenate([wo[:, :128], wo[:, 128:]], axis=0)
    first = core == 0
    gath[core, y, zl, x, 64:80, :] = jnp.where(first, aux_0, aux_1).astype(BF)

    pl.semaphore_wait(barrier, len(partners))

    used = [0]
    begun = []

    def send(src, dst, dev):
        k = used[0]
        used[0] += 1
        c = pltpu.make_async_remote_copy(
            src_ref=src,
            dst_ref=dst,
            send_sem=send_sem.at[k],
            recv_sem=recv_sem.at[k],
            device_id=dev,
            device_id_type=pl.DeviceIdType.MESH,
        )
        c.start()
        begun.append(c)
        return c

    def mask_rows():
        loads[8].wait()
        loads[9].wait()
        pos = iota((SEQ, 1024), 0)
        for e in range(8):
            live = (len_c if e < 4 else len_p)[e % 4]
            rows = cot[e * SEQ : (e + 1) * SEQ, :].astype(F32)
            masked[e * SEQ : (e + 1) * SEQ, :] = jnp.where(pos < live, rows, 0.0).astype(BF)

    every = slice(None)
    ring = lambda p, n: lax.rem(p + n, n)

    def rows_a(p, zq, xs=every):
        return gath.at[core, p, zq, xs, pl.ds(0, 32)]

    def rows_b(lo, n, zq, xq):
        return gath.at[core, pl.ds(lo, n), zq, xq, pl.ds(32, 48)]

    swaps = []

    def swap(ref):
        swaps.append(send(ref, ref, at(other=True)))

    def out(ref, **d):
        return send(ref, ref, at(**d))

    def arrived(*copies):
        for c in copies:
            c.wait_recv()

    def a_plane(zq):
        ref = rows_a(y, zq)
        swap(ref)
        return zq, {d: out(ref, dy=d) for d in (2, -2, 1, -1)}

    def a_forward(chunk):
        zq, flying = chunk
        on = {}
        for sign, xs in ((1, pl.ds(0, 2)), (-1, pl.ds(2, 2))):
            p = ring(y - 2 * sign, NY)
            arrived(flying[2 * sign])
            on[sign] = (out(rows_a(p, zq, xs), dy=2 * sign), out(rows_a(p, zq), dy=sign))
            swap(rows_a(p, zq))
        return zq, on

    def a_near(chunk):
        zq, flying = chunk
        for sign in (1, -1):
            arrived(flying[sign])
            swap(rows_a(ring(y - sign, NY), zq))

    def a_far(chunk):
        zq, on = chunk
        for sign in (1, -1):
            arrived(on[sign][1])
            swap(rows_a(ring(y - 3 * sign, NY), zq))
        arrived(on[1][0], on[-1][0])
        swap(rows_a(ring(y + 4, NY), zq))

    def over_z(lo, zq, xq):
        ref = rows_b(lo, 4, zq, xq)
        return (
            out(ref, dz=1),
            out(ref, dz=-1),
            out(rows_b(lo, 2, zq, xq), dz=2),
            out(rows_b(lo + 2, 2, zq, xq), dz=-2),
        )

    def over_x(lo, zq, xq):
        ref = rows_b(lo, 4, zq, xq)
        return tuple(out(ref, dx=d) for d in (2, 1, 3))

    z_from = (ring(zl - 1, NZ), ring(zl + 1, NZ), ring(zl + 2, NZ))
    x_from = (ring(x - 2, NX), ring(x - 1, NX), ring(x - 3, NX))

    own_a = rows_a(y, zl, x)
    own_b = gath.at[core, y, zl, x, pl.ds(32, 48)]
    a1 = [out(own_a, dx=d) for d in (2, 1, 3)]
    b1 = [out(own_b, dy=d) for d in (4, 3, 5, 2, 6, 1, 7)]
    mask_rows()
    arrived(*a1)
    mine = rows_a(y, zl)
    a2 = (
        out(mine, dz=1),
        out(mine, dz=-1),
        out(rows_a(y, zl, pl.ds(0, 2)), dz=2),
        out(rows_a(y, zl, pl.ds(2, 2)), dz=-2),
    )
    chunk0 = a_plane(zl)
    arrived(*b1)
    bx2 = over_z(0, zl, x)
    bz2 = over_x(4, zl, x)
    bx3 = [(zl, over_x(0, zl, x))]
    bz3 = [(x, over_z(4, zl, x))]
    swap(rows_b(0, 8, zl, x))
    arrived(a2[0])
    chunk1 = a_plane(z_from[0])
    arrived(a2[1])
    chunk2 = a_plane(z_from[1])
    arrived(a2[2], a2[3])
    chunk3 = a_plane(z_from[2])
    far = [a_forward(chunk0)]
    a_near(chunk0)

    def bx_next(zq):
        bx3.append((zq, over_x(0, zq, x)))
        swap(rows_b(0, 4, zq, x))

    def bz_next(xq):
        bz3.append((xq, over_z(4, zl, xq)))
        swap(rows_b(4, 4, zl, xq))

    for k in range(2):
        arrived(bx2[k])
        bx_next(z_from[k])
        arrived(bz2[1 + k])
        bz_next(x_from[1 + k])
    arrived(bz2[0])
    bz_next(x_from[0])
    arrived(bx2[2], bx2[3])
    bx_next(z_from[2])
    for chunk in (chunk1, chunk2, chunk3):
        far.append(a_forward(chunk))
        a_near(chunk)

    def b_last(k):
        zq, flying = bx3[k]
        for c, xq in zip(flying, x_from):
            arrived(c)
            swap(rows_b(0, 4, zq, xq))
        xq, flying = bz3[k]
        arrived(flying[0])
        swap(rows_b(4, 4, z_from[0], xq))
        arrived(flying[1])
        swap(rows_b(4, 4, z_from[1], xq))
        arrived(flying[2], flying[3])
        swap(rows_b(4, 4, z_from[2], xq))

    for k in range(4):
        b_last(k)
        a_far(far[k])
    loads[10].wait()
    loads[11].wait()
    for c in swaps:
        c.wait_recv()

    low = iota((8, 8, 128), 2) < 64

    def plane(k, acc):
        inward, right_sum, grad, outward = acc
        lanes = pl.ds(pl.multiple_of(k * 1024, 1024), 1024)
        xk = xs[:, lanes]
        w = jnp.concatenate(
            [gath[h, k, :, :, 0:64, :].reshape(1024, 128) for h in range(2)], axis=1
        )
        inward = inward + nn(xk, w)
        a0 = gath[0, k, :, :, 64:80, :].reshape(16, 16, 128).astype(F32)
        a1 = gath[1, k, :, :, 64:80, :].reshape(16, 16, 128).astype(F32)
        wo_k = jnp.concatenate(
            [a0[:, 0:8].reshape(128, 128), a0[:, 8:16].reshape(128, 128)], axis=1
        ).astype(BF)
        up_k = a1[:, 8:16].reshape(128, 128).astype(BF)
        pairs = a1[:, 0:8].reshape(8, 2, 8, 128)
        te, to = pairs[:, 0], pairs[:, 1]
        t8 = jnp.where(low, te, to)
        b8 = pltpu.roll(jnp.where(low, to, te), 64, 2)
        fold_t = jnp.concatenate(
            [jnp.concatenate([t8[m], b8[m]], axis=0) for m in range(8)], axis=1
        ).astype(BF)
        right_sum = right_sum + nt(xk, fold_t)
        mk = masked[:, pl.ds(pl.multiple_of(k * 128, 128), 128)]
        grad = grad + nn(mk, up_k)
        outward = outward + nn(mk, wo_k)
        return inward, right_sum, grad, outward

    zeros = lambda n: jnp.zeros((256, n), F32)
    inward, right_sum, grad, outward = lax.fori_loop(
        0, NY, plane, (zeros(256), zeros(16), zeros(128), zeros(256))
    )

    own = lax.rem(iota((128, 256), 0), 8) == iota((128, 256), 1) // SEQ
    spread_k = one_hot_rows(128, 16, 8)
    rd = nn(spread_k, rk_down[...]).astype(BF)
    left_t = jnp.where(own, nt(rd, grad.astype(BF)), 0.0).astype(BF)
    right_t = jnp.where(own, nt(spread_k, right_sum.astype(BF)), 0.0).astype(BF)
    gl = nn(left_t, inward.astype(BF))
    gr = nn(right_t, outward.astype(BF))
    joined = jnp.concatenate(
        [g[8 * k : 8 * k + 8] for g in (gl, gr) for k in range(16)], axis=1
    )
    inv = lax.rsqrt(jnp.sum(joined * joined, axis=1, keepdims=True) / 8192.0 + EPS)
    normed = joined * inv
    feats[...] = normed.astype(BF)

    for b in range(NY):
        part = normed[:, 1024 * b : 1024 * b + 1024]
        spread[b] = jnp.concatenate([part[:, :512], part[:, 512:]], axis=0).astype(BF)
    taken[y] = spread[y]
    moved = [
        send(spread.at[lax.rem(y + d, NY)], taken.at[y], at(dy=d)) for d in (4, 3, 5, 2, 6, 1, 7)
    ]
    for c in moved:
        c.wait_recv()
    upper = iota((8, 1024), 0) < 4
    f_rows, p_rows = [], []
    for m in range(4):
        a, b = (
            jnp.concatenate([v[0:8], v[8:16]], axis=1)
            for v in (taken[2 * m].astype(F32), taken[2 * m + 1].astype(F32))
        )
        f_rows.append(jnp.where(upper, a, pltpu.roll(b, 4, 0)))
        p_rows.append(jnp.where(upper, pltpu.roll(a, 4, 0), b))
    fblk[zl] = jnp.concatenate(f_rows, axis=0).astype(BF)
    pblk[x] = jnp.concatenate(p_rows, axis=0).astype(BF)
    moved = []
    for d in range(1, NZ):
        moved.append(send(fblk.at[zl], fblk.at[zl], at(z_in=lax.rem(zl + d, NZ))))
    for d in (2, 1, 3):
        moved.append(send(pblk.at[x], pblk.at[x], at(dx=d)))
    for c in moved:
        c.wait_recv()
    prod = nt(fblk[...].reshape(128, 1024), pblk[...].reshape(128, 1024))

    upper = iota((8, 128), 0) < 4
    tile = lambda zq, m: prod[zq * 32 + m * 8 : zq * 32 + m * 8 + 8]
    for m in range(4):
        for h in range(2):
            a, b = tile(2 * h, m), tile(2 * h + 1, m)
            tsum[2 * m, 8 * h : 8 * h + 8] = jnp.where(upper, a, pltpu.roll(b, 4, 0))
            tsum[2 * m + 1, 8 * h : 8 * h + 8] = jnp.where(upper, pltpu.roll(a, 4, 0), b)
    tgot[y] = tsum[y]
    moved = [
        send(tsum.at[lax.rem(y + d, NY)], tgot.at[y], at(dy=d)) for d in (4, 3, 5, 2, 6, 1, 7)
    ]
    for c in moved:
        c.wait_recv()
    total = tgot[0]
    for k in range(1, NY):
        total = total + tgot[k]
    vsum[0] = total[0:8]
    vsum[1] = total[8:16]
    vgot[zl] = vsum[zl // 2]
    moved = []
    for d in range(1, NZ):
        tz = lax.rem(zl + d, NZ)
        moved.append(send(vsum.at[tz // 2], vgot.at[zl], at(z_in=tz)))

    src, col = iota((512, 512), 0), iota((512, 512), 1)
    want = ((col // 16) % 4) * 128 + ((col // 4) % 4) * 32 + (col // 64) * 4 + col % 4
    perm = (src == want).astype(F32).astype(BF)
    for c in moved:
        c.wait_recv()
    odd_z = lax.rem(zl, 2) == 1
    flat = jnp.concatenate(
        [jnp.where(odd_z, pltpu.roll(vgot[k], 4, 0), vgot[k]) for k in range(NZ)], axis=1
    )
    p1 = flat.astype(BF)
    rest = flat - p1.astype(F32)
    p2 = rest.astype(BF)
    p3 = (rest - p2.astype(F32)).astype(BF)
    out = nn(p1, perm) + nn(p2, perm) + nn(p3, perm)
    scores[...] = out * (1.0 / 8192.0)

    for c in begun:
        c.wait_send()


def body(xc, ct_c, len_c, xp, ct_p, len_p, down, up, win, wout, rk_down, rk_up):
    width, values = xc.shape[2], ct_c.shape[2]
    anyspace = pl.BlockSpec(memory_space=pl.ANY)
    vmem = pl.BlockSpec(memory_space=pltpu.VMEM)
    scores, feats = pl.pallas_call(
        kernel,
        out_shape=(
            jax.ShapeDtypeStruct((8, 512), F32),
            jax.ShapeDtypeStruct((8, 8192), BF),
        ),
        in_specs=[anyspace] * 12,
        out_specs=(vmem, vmem),
        scratch_shapes=[
            pltpu.SMEM((4,), jnp.int32),
            pltpu.SMEM((4,), jnp.int32),
            pltpu.VMEM((64, 128), BF),
            pltpu.VMEM((8, 128), BF),
            pltpu.VMEM((8, 256), BF),
            pltpu.VMEM((16, 128), BF),
            pltpu.VMEM((16, 128), BF),
            pltpu.VMEM((2, NY, NZ, NX, 80, 128), BF),
            pltpu.VMEM((256, 8192), BF),
            pltpu.VMEM((256, 1024), BF),
            pltpu.VMEM((256, 1024), BF),
            pltpu.VMEM((NY, 16, 512), BF),
            pltpu.VMEM((NY, 16, 512), BF),
            pltpu.VMEM((NZ, 32, 1024), BF),
            pltpu.VMEM((NX, 32, 1024), BF),
            pltpu.VMEM((NY, 16, 128), F32),
            pltpu.VMEM((NY, 16, 128), F32),
            pltpu.VMEM((2, 8, 128), F32),
            pltpu.VMEM((NZ, 8, 128), F32),
            pltpu.SemaphoreType.DMA((12,)),
            pltpu.SemaphoreType.DMA((N_SEMS,)),
            pltpu.SemaphoreType.DMA((N_SEMS,)),
        ],
        compiler_params=pltpu.CompilerParams(
            collective_id=0, has_side_effects=True, vmem_limit_bytes=67043328
        ),
        name="lora_scores",
    )(
        xc.reshape(-1, width), ct_c.reshape(-1, values), len_c,
        xp.reshape(-1, width), ct_p.reshape(-1, values), len_p,
        down, up, win, wout, rk_down.T, rk_up.T,
    )
    return scores[:4], feats[:4]


def solution(mesh):
    split = Mesh(mesh.devices.reshape(NY, NZ, NX, 2, 2), AXES)
    rows = P(FSDP, None)
    whole = P(DP_FSDP, None, None)
    return jax.shard_map(
        body,
        mesh=split,
        in_specs=(
            whole, whole, P(DP_FSDP), whole, whole, P(DP_FSDP), rows, rows, rows, rows, P(), P(),
        ),
        out_specs=(P(DP_FSDP, None), P(DP_FSDP, None)),
        check_vma=False,
    )
```

```python
import jax
import jax.numpy as jnp
from jax import lax
from jax.experimental import pallas as pl
from jax.experimental.pallas import tpu as pltpu
from jax.sharding import Mesh
from jax.sharding import PartitionSpec as P

AXES = ("y", "zl", "x", "zh", "core")
FSDP = ("y", "zl", "x")
DP_FSDP = ("zh", "core", "y", "zl", "x")
NY, NZ, NX = 8, 4, 4
SEQ = 32
EPS = 1e-06
BF, F32 = jnp.bfloat16, jnp.float32

N_SEND, N_RECV = 13, 47


def nt(a, b):
    return lax.dot_general(a, b, (((1,), (1,)), ((), ())), preferred_element_type=F32)


def nn(a, b):
    return jnp.dot(a, b, preferred_element_type=F32)


def iota(shape, dim):
    return lax.broadcasted_iota(jnp.int32, shape, dim)


def one_hot_rows(rows, cols, per):
    return (iota((rows, cols), 0) // per == iota((rows, cols), 1)).astype(F32).astype(BF)


def kernel(
    xc, ct_c, len_ch, xp, ct_p, len_ph, down_h, up_h, win_h, wout_h, rk_down_h, rk_up_h,
    scores, feats,
    len_c, len_p, down, up, wout, rk_down, rk_up,
    gath, xs, cot, masked, f_out, p_out, fblk, pblk, tsum, tgot, vsum, vgot, perm,
    ld_sem, send_sem, recv_sem,
):
    y, zl, x = (lax.axis_index(a) for a in FSDP)
    zh, core = lax.axis_index("zh"), lax.axis_index("core")
    zz = zh * NZ + zl

    def at(dy=0, dx=0, dz=0, z_in=None, other=False):
        if z_in is None:
            full = lax.rem(zz + dz + 8, 8)
            tz, th = lax.rem(full, NZ), full // NZ
        else:
            tz, th = z_in, zh
        return (
            lax.rem(y + dy + NY, NY),
            tz,
            lax.rem(x + dx + NX, NX),
            th,
            1 - core if other else core,
        )

    loads = [
        pltpu.make_async_copy(src, dst, ld_sem.at[k])
        for k, (src, dst) in enumerate(
            (
                (win_h.at[:, pl.ds(pl.multiple_of(core * 128, 128), 128)], gath.at[core, y, zl, x, pl.ds(0, 64)]),
                (rk_up_h, rk_up),
                (down_h, down),
                (up_h, up),
                (wout_h, wout),
                (rk_down_h, rk_down),
                (len_ch, len_c),
                (len_ph, len_p),
                (ct_c, cot.at[pl.ds(0, 128)]),
                (ct_p, cot.at[pl.ds(128, 128)]),
                (xc, xs.at[pl.ds(0, 128)]),
                (xp, xs.at[pl.ds(128, 128)]),
            )
        )
    ]
    for c in loads:
        c.start()

    barrier = pltpu.get_barrier_semaphore()
    partners = [at(dy=d) for d in range(1, NY)] + [at(dx=d) for d in range(1, NX)]
    partners += [at(z_in=lax.rem(zl + d, NZ)) for d in range(1, NZ)]
    partners += [at(dz=d) for d in (1, -1, 2, -2)] + [at(other=True)]
    for dev in partners:
        pl.semaphore_signal(barrier, inc=1, device_id=dev, device_id_type=pl.DeviceIdType.MESH)

    loads[0].wait()
    pl.semaphore_wait(barrier, len(partners))

    names = {}

    def key(kind, name):
        return names.setdefault(kind, {}).setdefault(name, len(names.get(kind, {})))

    def send(src, dst, dev, group, arrival):
        pltpu.make_async_remote_copy(
            src_ref=src,
            dst_ref=dst,
            send_sem=send_sem.at[key("send", group)],
            recv_sem=recv_sem.at[key("recv", arrival)],
            device_id=dev,
            device_id_type=pl.DeviceIdType.MESH,
        ).start()

    def arrived(arrival, ref):
        pltpu.make_async_copy(ref, ref, recv_sem.at[key("recv", arrival)]).wait()

    def left(group, ref):
        pltpu.make_async_copy(ref, ref, send_sem.at[key("send", group)]).wait()

    def mask_rows():
        loads[8].wait()
        loads[9].wait()
        pos = iota((SEQ, 1024), 0)
        for e in range(8):
            live = (len_c if e < 4 else len_p)[e % 4]
            rows = cot[e * SEQ : (e + 1) * SEQ, :].astype(F32)
            masked[e * SEQ : (e + 1) * SEQ, :] = jnp.where(pos < live, rows, 0.0).astype(BF)

    every = slice(None)
    ring = lambda p, n: lax.rem(p + n, n)

    def rows_a(p, zq, xs=every):
        return gath.at[core, p, zq, xs, pl.ds(0, 32)]

    def rows_b(lo, n, zq, xq):
        return gath.at[core, pl.ds(lo, n), zq, xq, pl.ds(32, 48)]

    def swap(ref):
        send(ref, ref, at(other=True), "swap", "swap")

    def out(ref, group, arrival, **d):
        send(ref, ref, at(**d), group, arrival)

    def a_plane(zq, c):
        ref = rows_a(y, zq)
        swap(ref)
        for d in (2, -2):
            out(ref, "plane", ("two", c, d), dy=d)
        for d in (1, -1):
            out(ref, "plane", ("near", c), dy=d)

    def a_forward(zq, c):
        for sign, lo in ((1, 0), (-1, 2)):
            ref = rows_a(ring(y - 2 * sign, NY), zq)
            arrived(("two", c, 2 * sign), ref)
            out(rows_a(ring(y - 2 * sign, NY), zq, pl.ds(lo, 2)), "forward", ("far", c), dy=2 * sign)
            out(ref, "forward", ("far", c), dy=sign)
            swap(ref)

    def a_near(zq, c):
        arrived(("near", c), gath.at[core, pl.ds(0, 2), zq, :, pl.ds(0, 32)])
        for d in (1, -1):
            swap(rows_a(ring(y + d, NY), zq))

    def a_far(zq, c):
        arrived(("far", c), gath.at[core, pl.ds(0, 3), zq, :, pl.ds(0, 32)])
        for d in (3, -3, 4):
            swap(rows_a(ring(y + d, NY), zq))

    def over_z(lo, zq, xq, group, arrivals):
        ref = rows_b(lo, 4, zq, xq)
        out(ref, group, arrivals[0], dz=1)
        out(ref, group, arrivals[1], dz=-1)
        out(rows_b(lo, 2, zq, xq), group, arrivals[2], dz=2)
        out(rows_b(lo + 2, 2, zq, xq), group, arrivals[2], dz=-2)

    def over_x(lo, zq, xq, group, arrivals):
        ref = rows_b(lo, 4, zq, xq)
        for d, name in zip((2, 1, 3), arrivals):
            out(ref, group, name, dx=d)

    z_from = (ring(zl - 1, NZ), ring(zl + 1, NZ), ring(zl + 2, NZ))
    x_from = (ring(x - 2, NX), ring(x - 1, NX), ring(x - 3, NX))

    own_a = rows_a(y, zl, x)
    own_b = gath.at[core, y, zl, x, pl.ds(32, 32)]
    own_c = gath.at[core, y, zl, x, pl.ds(64, 16)]
    for d in (2, 1, 3):
        out(own_a, "a1", "a1", dx=d)
    for d in (4, 3, 5, 2, 6, 1, 7):
        out(own_b, "b1", "b1", dy=d)
    for c in loads[1:8]:
        c.wait()
    ru = rk_up[...].astype(F32)
    top, bottom = ru[0:8], ru[8:16]
    odd = lax.rem(x, 2) == 1
    one = jnp.where(odd, bottom, top)
    two = jnp.where(odd, top, bottom)
    dn = down[...]
    zero = jnp.zeros_like(dn)
    wide = jnp.concatenate(
        [jnp.concatenate([dn, zero], axis=1), jnp.concatenate([zero, dn], axis=1)], axis=0
    )
    fold = nt(jnp.concatenate([one, two], axis=1).astype(BF), wide)
    aux_1 = jnp.concatenate([fold, up[...].astype(F32)], axis=0)
    wo = wout[...].astype(F32)
    aux_0 = jnp.concatenate([wo[:, :128], wo[:, 128:]], axis=0)
    first = core == 0
    gath[core, y, zl, x, 64:80, :] = jnp.where(first, aux_0, aux_1).astype(BF)
    for d in (4, 3, 5, 2, 6, 1, 7):
        out(own_c, "b1", "b1", dy=d)
    mask_rows()
    arrived("a1", gath.at[core, y, zl, pl.ds(0, 3), pl.ds(0, 32)])
    mine = rows_a(y, zl)
    out(mine, "a2", "a2-", dz=1)
    out(mine, "a2", "a2+", dz=-1)
    out(rows_a(y, zl, pl.ds(0, 2)), "a2", "a2=", dz=2)
    out(rows_a(y, zl, pl.ds(2, 2)), "a2", "a2=", dz=-2)
    a_plane(zl, 0)
    src, col = iota((512, 512), 0), iota((512, 512), 1)
    want = ((col >> 4) & 3) * 128 + ((col >> 2) & 3) * 32 + (col >> 6) * 4 + (col & 3)
    perm[...] = (src == want).astype(F32).astype(BF)
    arrived("b1", gath.at[core, pl.ds(0, 7), zl, x, pl.ds(32, 48)])
    over_z(0, zl, x, "b2", ("bx2-", "bx2+", "bx2="))
    over_x(4, zl, x, "b2", ("bz2a", "bz2b", "bz2c"))
    over_x(0, zl, x, "b3", (("bx3", 0),) * 3)
    over_z(4, zl, x, "b3", (("bz3", 0),) * 3)
    swap(rows_b(0, 8, zl, x))
    for c, name in enumerate(("a2-", "a2+", "a2=")):
        arrived(name, rows_a(y, z_from[c]))
        a_plane(z_from[c], c + 1)
    a_forward(zl, 0)
    a_near(zl, 0)

    def bx_next(c, name):
        zq = z_from[c]
        arrived(name, rows_b(0, 4, zq, x))
        over_x(0, zq, x, "b3", (("bx3", c + 1),) * 3)
        swap(rows_b(0, 4, zq, x))

    def bz_next(c, name):
        xq = x_from[c]
        arrived(name, rows_b(4, 4, zl, xq))
        over_z(4, zl, xq, "b3", (("bz3", c + 1),) * 3)
        swap(rows_b(4, 4, zl, xq))

    bx_next(0, "bx2-")
    bz_next(1, "bz2b")
    bx_next(1, "bx2+")
    bz_next(2, "bz2c")
    bz_next(0, "bz2a")
    bx_next(2, "bx2=")
    for c in range(3):
        a_forward(z_from[c], c + 1)
        a_near(z_from[c], c + 1)
    bz_order = (x, x_from[0], x_from[1], x_from[2])
    for c, zq in enumerate((zl,) + z_from):
        arrived(("bx3", c), gath.at[core, pl.ds(0, 4), zq, pl.ds(0, 3), pl.ds(32, 48)])
        for xq in x_from:
            swap(rows_b(0, 4, zq, xq))
        xq = bz_order[c]
        arrived(("bz3", c), gath.at[core, pl.ds(4, 4), pl.ds(0, 3), xq, pl.ds(32, 48)])
        for zr in z_from:
            swap(rows_b(4, 4, zr, xq))
        a_far(zq, c)
    loads[10].wait()
    loads[11].wait()
    arrived("swap", gath.at[1 - core])

    low = iota((8, 8, 128), 2) < 64

    def plane(k, acc):
        inward_c, inward_p, right_t, grad, outward = acc
        lanes = pl.ds(pl.multiple_of(k * 1024, 1024), 1024)
        xk = xs[:, lanes]
        w = jnp.concatenate(
            [gath[h, k, :, :, 0:64, :].reshape(1024, 128) for h in range(2)], axis=1
        )
        inward_c = inward_c + nn(xk[:128], w)
        inward_p = inward_p + nn(xk[128:], w)
        a0 = gath[0, k, :, :, 64:80, :].reshape(16, 16, 128).astype(F32)
        a1 = gath[1, k, :, :, 64:80, :].reshape(16, 16, 128).astype(F32)
        wo_k = jnp.concatenate(
            [a0[:, 0:8].reshape(128, 128), a0[:, 8:16].reshape(128, 128)], axis=1
        ).astype(BF)
        up_k = a1[:, 8:16].reshape(128, 128).astype(BF)
        pairs = a1[:, 0:8].reshape(8, 2, 8, 128)
        te, to = pairs[:, 0], pairs[:, 1]
        t8 = jnp.where(low, te, to)
        b8 = pltpu.roll(jnp.where(low, to, te), 64, 2)
        fold_t = jnp.concatenate(
            [jnp.concatenate([t8[m], b8[m]], axis=0) for m in range(8)], axis=1
        ).astype(BF)
        right_t = right_t + nt(fold_t, xk)
        mk = masked[:, pl.ds(pl.multiple_of(k * 128, 128), 128)]
        grad = grad + nn(mk, up_k)
        outward = outward + nn(mk, wo_k)
        return inward_c, inward_p, right_t, grad, outward

    zeros = lambda m, n: jnp.zeros((m, n), F32)
    inward_c, inward_p, right_t, grad, outward = lax.fori_loop(
        0, NY, plane, (zeros(128, 256), zeros(128, 256), zeros(16, 256), zeros(256, 128), zeros(256, 256))
    )

    own = lax.rem(iota((128, 256), 0), 8) == iota((128, 256), 1) // SEQ
    spread_k = one_hot_rows(128, 16, 8)
    rd = nn(spread_k, rk_down[...]).astype(BF)
    left_t = jnp.where(own, nt(rd, grad.astype(BF)), 0.0).astype(BF)
    right_t = jnp.where(own, nn(spread_k, right_t.astype(BF)), 0.0).astype(BF)
    gl = nn(left_t, jnp.concatenate([inward_c, inward_p], axis=0).astype(BF))
    gr = nn(right_t, outward.astype(BF))
    joined = jnp.concatenate(
        [g[8 * k : 8 * k + 8] for g in (gl, gr) for k in range(16)], axis=1
    )
    inv = lax.rsqrt(jnp.sum(joined * joined, axis=1, keepdims=True) / 8192.0 + EPS)
    normed = joined * inv
    feats[...] = normed.astype(BF)

    upper = iota((8, 512), 0) < 4
    for b in range(NY):
        lo = normed[:, 1024 * b : 1024 * b + 512]
        hi = normed[:, 1024 * b + 512 : 1024 * b + 1024]
        f_out[b] = jnp.where(upper, lo, pltpu.roll(hi, 4, 0)).astype(BF)
        p_out[b] = jnp.where(upper, pltpu.roll(lo, 4, 0), hi).astype(BF)
    for d in (4, 3, 5, 2, 6, 1, 7):
        to = lax.rem(y + d, NY)
        send(f_out.at[to], fblk.at[zl, y], at(dy=d), "feature", ("piece", d))
        send(p_out.at[to], pblk.at[x, y], at(dy=d), "feature", ("piece", d))
    fblk[zl, y] = f_out[y]
    pblk[x, y] = p_out[y]

    def pass_on(p):
        f, q = fblk.at[zl, p], pblk.at[x, p]
        for d in (3, 2, 1):
            send(f, f, at(z_in=lax.rem(zl + d, NZ)), "cands", "cands")
        for d in (2, 1, 3):
            send(q, q, at(dx=d), "probes", "probes")

    pass_on(y)
    for d in (1, 7, 2, 6, 3, 5, 4):
        arrived(("piece", d), f_out.at[pl.ds(0, 2)])
        pass_on(ring(y - d, NY))
    arrived("cands", fblk.at[pl.ds(0, 3)])
    arrived("probes", pblk.at[pl.ds(0, 3)])

    def halves(ref):
        lo, hi = [], []
        for k in range(4):
            for m in range(4):
                a, b = ref[k, 2 * m].astype(F32), ref[k, 2 * m + 1].astype(F32)
                lo.append(jnp.where(upper, a, pltpu.roll(b, 4, 0)))
                hi.append(jnp.where(upper, pltpu.roll(a, 4, 0), b))
        return tuple(jnp.concatenate(v, axis=0).astype(BF) for v in (lo, hi))

    f_lo, f_hi = halves(fblk)
    p_lo, p_hi = halves(pblk)
    prod = nt(f_lo, p_lo) + nt(f_hi, p_hi)

    upper = iota((8, 128), 0) < 4
    tile = lambda zq, m: prod[zq * 32 + m * 8 : zq * 32 + m * 8 + 8]
    for m in range(4):
        for h in range(2):
            a, b = tile(2 * h, m), tile(2 * h + 1, m)
            tsum[2 * m, 8 * h : 8 * h + 8] = jnp.where(upper, a, pltpu.roll(b, 4, 0))
            tsum[2 * m + 1, 8 * h : 8 * h + 8] = jnp.where(upper, pltpu.roll(a, 4, 0), b)
    tgot[y] = tsum[y]
    for d in (4, 3, 5, 2, 6, 1, 7):
        send(tsum.at[lax.rem(y + d, NY)], tgot.at[y], at(dy=d), "sums", "sums")
    arrived("sums", tgot.at[pl.ds(0, 7)])
    total = tgot[0]
    for k in range(1, NY):
        total = total + tgot[k]
    vsum[0] = total[0:8]
    vsum[1] = total[8:16]
    vgot[zl] = vsum[zl // 2]
    for d in range(1, NZ):
        tz = lax.rem(zl + d, NZ)
        send(vsum.at[tz // 2], vgot.at[zl], at(z_in=tz), "rows", "rows")
    arrived("rows", vgot.at[pl.ds(0, 3)])
    odd_z = lax.rem(zl, 2) == 1
    flat = jnp.concatenate(
        [jnp.where(odd_z, pltpu.roll(vgot[k], 4, 0), vgot[k]) for k in range(NZ)], axis=1
    )
    p1 = flat.astype(BF).astype(F32)
    p2 = (flat - p1).astype(BF).astype(F32)
    pieces = nn(jnp.concatenate([p1, p2, flat - p1 - p2], axis=0).astype(BF), perm[...])
    out_rows = pieces[0:8] + pieces[8:16] + pieces[16:24]
    scores[...] = out_rows * (1.0 / 8192.0)

    for group, ref in (
        ("a1", gath.at[core, y, zl, pl.ds(0, 3), pl.ds(0, 32)]),
        ("b1", gath.at[core, pl.ds(0, 7), zl, x, pl.ds(32, 48)]),
        ("a2", gath.at[core, y, pl.ds(0, 3), :, pl.ds(0, 32)]),
        ("plane", gath.at[core, pl.ds(0, 4), :, :, pl.ds(0, 32)]),
        ("forward", gath.at[core, pl.ds(0, 3), :, :, pl.ds(0, 32)]),
        ("b2", gath.at[core, pl.ds(0, 6), :, x, pl.ds(32, 48)]),
        ("b3", gath.at[core, pl.ds(0, 6), :, :, pl.ds(32, 48)]),
        ("swap", gath.at[core]),
        ("feature", fblk.at[pl.ds(0, 2), pl.ds(0, 7)]),
        ("cands", fblk.at[pl.ds(0, 3)]),
        ("probes", pblk.at[pl.ds(0, 3)]),
        ("sums", tsum.at[pl.ds(0, 7)]),
        ("rows", vgot.at[pl.ds(0, 3)]),
    ):
        left(group, ref)
    assert len(names["send"]) == N_SEND and len(names["recv"]) == N_RECV, names


def own_rows(scores, feats, own_scores, own_feats):
    own_scores[...] = scores[0:4]
    own_feats[...] = feats[0:4]


def body(xc, ct_c, len_c, xp, ct_p, len_p, down, up, win, wout, rk_down, rk_up):
    width, values = xc.shape[2], ct_c.shape[2]
    anyspace = pl.BlockSpec(memory_space=pl.ANY)
    vmem = pl.BlockSpec(memory_space=pltpu.VMEM)
    scores, feats = pl.pallas_call(
        kernel,
        out_shape=(
            jax.ShapeDtypeStruct((8, 512), F32),
            jax.ShapeDtypeStruct((8, 8192), BF),
        ),
        in_specs=[anyspace] * 12,
        out_specs=(vmem, vmem),
        scratch_shapes=[
            pltpu.SMEM((4,), jnp.int32),
            pltpu.SMEM((4,), jnp.int32),
            pltpu.VMEM((64, 128), BF),
            pltpu.VMEM((8, 128), BF),
            pltpu.VMEM((8, 256), BF),
            pltpu.VMEM((16, 128), BF),
            pltpu.VMEM((16, 128), BF),
            pltpu.VMEM((2, NY, NZ, NX, 80, 128), BF),
            pltpu.VMEM((256, 8192), BF),
            pltpu.VMEM((256, 1024), BF),
            pltpu.VMEM((256, 1024), BF),
            pltpu.VMEM((NY, 8, 512), BF),
            pltpu.VMEM((NY, 8, 512), BF),
            pltpu.VMEM((NZ, NY, 8, 512), BF),
            pltpu.VMEM((NX, NY, 8, 512), BF),
            pltpu.VMEM((NY, 16, 128), F32),
            pltpu.VMEM((NY, 16, 128), F32),
            pltpu.VMEM((2, 8, 128), F32),
            pltpu.VMEM((NZ, 8, 128), F32),
            pltpu.VMEM((512, 512), BF),
            pltpu.SemaphoreType.DMA((12,)),
            pltpu.SemaphoreType.DMA((N_SEND,)),
            pltpu.SemaphoreType.DMA((N_RECV,)),
        ],
        compiler_params=pltpu.CompilerParams(
            collective_id=0, has_side_effects=True, vmem_limit_bytes=67043328
        ),
        name="lora_scores",
    )(
        xc.reshape(-1, width), ct_c.reshape(-1, values), len_c,
        xp.reshape(-1, width), ct_p.reshape(-1, values), len_p,
        down, up, win, wout, rk_down.T, rk_up.T,
    )
    return pl.pallas_call(
        own_rows,
        out_shape=(
            jax.ShapeDtypeStruct((4, 512), F32),
            jax.ShapeDtypeStruct((4, 8192), BF),
        ),
        in_specs=[vmem, vmem],
        out_specs=(vmem, vmem),
        name="own_rows",
    )(scores, feats)


def solution(mesh):
    split = Mesh(mesh.devices.reshape(NY, NZ, NX, 2, 2), AXES)
    rows = P(FSDP, None)
    whole = P(DP_FSDP, None, None)
    return jax.shard_map(
        body,
        mesh=split,
        in_specs=(
            whole, whole, P(DP_FSDP), whole, whole, P(DP_FSDP), rows, rows, rows, rows, P(), P(),
        ),
        out_specs=(P(DP_FSDP, None), P(DP_FSDP, None)),
        check_vma=False,
    )
```

```python
import jax
import jax.numpy as jnp
from jax import lax
from jax.experimental import pallas as pl
from jax.experimental.pallas import tpu as pltpu
from jax.sharding import Mesh
from jax.sharding import PartitionSpec as P

AXES = ("y", "zl", "x", "zh", "core")
FSDP = ("y", "zl", "x")
DP_FSDP = ("zh", "core", "y", "zl", "x")
NY, NZ, NX = 8, 4, 4
SEQ = 32
EPS = 1e-06
BF, F32 = jnp.bfloat16, jnp.float32

N_SEND, N_RECV = 13, 47


def nt(a, b):
    return lax.dot_general(a, b, (((1,), (1,)), ((), ())), preferred_element_type=F32)


def nn(a, b):
    return jnp.dot(a, b, preferred_element_type=F32)


def iota(shape, dim):
    return lax.broadcasted_iota(jnp.int32, shape, dim)


def one_hot_rows(rows, cols, per):
    return (iota((rows, cols), 0) // per == iota((rows, cols), 1)).astype(F32).astype(BF)


def kernel(
    xc, ct_c, len_ch, xp, ct_p, len_ph, down_h, up_h, win_h, wout_h, rk_down_h, rk_up_h,
    scores, feats,
    len_c, len_p, down, up, wout, rk_down, rk_up,
    gath, xs, cot, masked, f_out, p_out, fblk, pblk, tsum, tgot, vsum, vgot, perm, out_w, fold_w,
    ld_sem, send_sem, recv_sem,
):
    y, zl, x = (lax.axis_index(a) for a in FSDP)
    zh, core = lax.axis_index("zh"), lax.axis_index("core")
    zz = zh * NZ + zl

    def at(dy=0, dx=0, dz=0, z_in=None, other=False):
        if z_in is None:
            full = lax.rem(zz + dz + 8, 8)
            tz, th = lax.rem(full, NZ), full // NZ
        else:
            tz, th = z_in, zh
        return (
            lax.rem(y + dy + NY, NY),
            tz,
            lax.rem(x + dx + NX, NX),
            th,
            1 - core if other else core,
        )

    loads = [
        pltpu.make_async_copy(src, dst, ld_sem.at[k])
        for k, (src, dst) in enumerate(
            (
                (win_h.at[:, pl.ds(pl.multiple_of(core * 128, 128), 128)], gath.at[core, y, zl, x, pl.ds(0, 64)]),
                (rk_up_h, rk_up),
                (down_h, down),
                (up_h, up),
                (wout_h, wout),
                (rk_down_h, rk_down),
                (len_ch, len_c),
                (len_ph, len_p),
                (ct_c, cot.at[pl.ds(0, 128)]),
                (ct_p, cot.at[pl.ds(128, 128)]),
                (xc, xs.at[pl.ds(0, 128)]),
                (xp, xs.at[pl.ds(128, 128)]),
            )
        )
    ]
    for c in loads:
        c.start()

    barrier = pltpu.get_barrier_semaphore()
    partners = [at(dy=d) for d in range(1, NY)] + [at(dx=d) for d in range(1, NX)]
    partners += [at(z_in=lax.rem(zl + d, NZ)) for d in range(1, NZ)]
    partners += [at(dz=d) for d in (1, -1, 2, -2)] + [at(other=True)]
    for dev in partners:
        pl.semaphore_signal(barrier, inc=1, device_id=dev, device_id_type=pl.DeviceIdType.MESH)

    loads[0].wait()
    pl.semaphore_wait(barrier, len(partners))

    names = {}

    def key(kind, name):
        return names.setdefault(kind, {}).setdefault(name, len(names.get(kind, {})))

    def send(src, dst, dev, group, arrival):
        pltpu.make_async_remote_copy(
            src_ref=src,
            dst_ref=dst,
            send_sem=send_sem.at[key("send", group)],
            recv_sem=recv_sem.at[key("recv", arrival)],
            device_id=dev,
            device_id_type=pl.DeviceIdType.MESH,
        ).start()

    def arrived(arrival, ref):
        pltpu.make_async_copy(ref, ref, recv_sem.at[key("recv", arrival)]).wait()

    def left(group, ref):
        pltpu.make_async_copy(ref, ref, send_sem.at[key("send", group)]).wait()

    def mask_rows():
        loads[8].wait()
        loads[9].wait()
        pos = iota((SEQ, 1024), 0)
        for e in range(8):
            live = (len_c if e < 4 else len_p)[e % 4]
            rows = cot[e * SEQ : (e + 1) * SEQ, :].astype(F32)
            masked[e * SEQ : (e + 1) * SEQ, :] = jnp.where(pos < live, rows, 0.0).astype(BF)

    every = slice(None)
    ring = lambda p, n: lax.rem(p + n, n)

    def rows_a(p, zq, xs=every):
        return gath.at[core, p, zq, xs, pl.ds(0, 32)]

    def rows_b(lo, n, zq, xq):
        return gath.at[core, pl.ds(lo, n), zq, xq, pl.ds(32, 48)]

    def swap(ref):
        send(ref, ref, at(other=True), "swap", "swap")

    def out(ref, group, arrival, **d):
        send(ref, ref, at(**d), group, arrival)

    def a_plane(zq, c):
        ref = rows_a(y, zq)
        swap(ref)
        for d in (2, -2):
            out(ref, "plane", ("two", c, d), dy=d)
        for d in (1, -1):
            out(ref, "plane", ("near", c), dy=d)

    def a_forward(zq, c):
        for sign, lo in ((1, 0), (-1, 2)):
            ref = rows_a(ring(y - 2 * sign, NY), zq)
            arrived(("two", c, 2 * sign), ref)
            out(rows_a(ring(y - 2 * sign, NY), zq, pl.ds(lo, 2)), "forward", ("far", c), dy=2 * sign)
            out(ref, "forward", ("far", c), dy=sign)
            swap(ref)

    def a_near(zq, c):
        arrived(("near", c), gath.at[core, pl.ds(0, 2), zq, :, pl.ds(0, 32)])
        for d in (1, -1):
            swap(rows_a(ring(y + d, NY), zq))

    def a_far(zq, c):
        arrived(("far", c), gath.at[core, pl.ds(0, 3), zq, :, pl.ds(0, 32)])
        for d in (3, -3, 4):
            swap(rows_a(ring(y + d, NY), zq))

    def over_z(lo, zq, xq, group, arrivals):
        ref = rows_b(lo, 4, zq, xq)
        out(ref, group, arrivals[0], dz=1)
        out(ref, group, arrivals[1], dz=-1)
        out(rows_b(lo, 2, zq, xq), group, arrivals[2], dz=2)
        out(rows_b(lo + 2, 2, zq, xq), group, arrivals[2], dz=-2)

    def over_x(lo, zq, xq, group, arrivals):
        ref = rows_b(lo, 4, zq, xq)
        for d, name in zip((2, 1, 3), arrivals):
            out(ref, group, name, dx=d)

    z_from = (ring(zl - 1, NZ), ring(zl + 1, NZ), ring(zl + 2, NZ))
    x_from = (ring(x - 2, NX), ring(x - 1, NX), ring(x - 3, NX))

    own_a = rows_a(y, zl, x)
    own_b = gath.at[core, y, zl, x, pl.ds(32, 32)]
    own_c = gath.at[core, y, zl, x, pl.ds(64, 16)]
    for d in (2, 1, 3):
        out(own_a, "a1", "a1", dx=d)
    for d in (4, 3, 5, 2, 6, 1, 7):
        out(own_b, "b1", "b1", dy=d)
    for c in loads[1:8]:
        c.wait()
    ru = rk_up[...].astype(F32)
    top, bottom = ru[0:8], ru[8:16]
    odd = lax.rem(x, 2) == 1
    one = jnp.where(odd, bottom, top)
    two = jnp.where(odd, top, bottom)
    dn = down[...]
    zero = jnp.zeros_like(dn)
    stacked = jnp.concatenate(
        [jnp.concatenate([dn, zero], axis=1), jnp.concatenate([zero, dn], axis=1)], axis=0
    )
    fold = nt(jnp.concatenate([one, two], axis=1).astype(BF), stacked)
    aux_1 = jnp.concatenate([fold, up[...].astype(F32)], axis=0)
    wo = wout[...].astype(F32)
    aux_0 = jnp.concatenate([wo[:, :128], wo[:, 128:]], axis=0)
    first = core == 0
    gath[core, y, zl, x, 64:80, :] = jnp.where(first, aux_0, aux_1).astype(BF)
    for d in (4, 3, 5, 2, 6, 1, 7):
        out(own_c, "b1", "b1", dy=d)
    mask_rows()
    arrived("a1", gath.at[core, y, zl, pl.ds(0, 3), pl.ds(0, 32)])
    mine = rows_a(y, zl)
    out(mine, "a2", "a2-", dz=1)
    out(mine, "a2", "a2+", dz=-1)
    out(rows_a(y, zl, pl.ds(0, 2)), "a2", "a2=", dz=2)
    out(rows_a(y, zl, pl.ds(2, 2)), "a2", "a2=", dz=-2)
    a_plane(zl, 0)
    src, col = iota((512, 512), 0), iota((512, 512), 1)
    want = ((col >> 4) & 3) * 128 + ((col >> 2) & 3) * 32 + (col >> 6) * 4 + (col & 3)
    perm[...] = (src == want).astype(F32).astype(BF)
    arrived("b1", gath.at[core, pl.ds(0, 7), zl, x, pl.ds(32, 48)])
    over_z(0, zl, x, "b2", ("bx2-", "bx2+", "bx2="))
    over_x(4, zl, x, "b2", ("bz2a", "bz2b", "bz2c"))
    over_x(0, zl, x, "b3", (("bx3", 0),) * 3)
    over_z(4, zl, x, "b3", (("bz3", 0),) * 3)
    swap(rows_b(0, 8, zl, x))
    for c, name in enumerate(("a2-", "a2+", "a2=")):
        arrived(name, rows_a(y, z_from[c]))
        a_plane(z_from[c], c + 1)
    a_forward(zl, 0)
    a_near(zl, 0)

    def bx_next(c, name):
        zq = z_from[c]
        arrived(name, rows_b(0, 4, zq, x))
        over_x(0, zq, x, "b3", (("bx3", c + 1),) * 3)
        swap(rows_b(0, 4, zq, x))

    def bz_next(c, name):
        xq = x_from[c]
        arrived(name, rows_b(4, 4, zl, xq))
        over_z(4, zl, xq, "b3", (("bz3", c + 1),) * 3)
        swap(rows_b(4, 4, zl, xq))

    bx_next(0, "bx2-")
    bz_next(1, "bz2b")
    bx_next(1, "bx2+")
    bz_next(2, "bz2c")
    bz_next(0, "bz2a")
    bx_next(2, "bx2=")
    for c in range(3):
        a_forward(z_from[c], c + 1)
        a_near(z_from[c], c + 1)
    bz_order = (x, x_from[0], x_from[1], x_from[2])
    for c, zq in enumerate((zl,) + z_from):
        arrived(("bx3", c), gath.at[core, pl.ds(0, 4), zq, pl.ds(0, 3), pl.ds(32, 48)])
        for xq in x_from:
            swap(rows_b(0, 4, zq, xq))
        xq = bz_order[c]
        arrived(("bz3", c), gath.at[core, pl.ds(4, 4), pl.ds(0, 3), xq, pl.ds(32, 48)])
        for zr in z_from:
            swap(rows_b(4, 4, zr, xq))
        a_far(zq, c)
    loads[10].wait()
    loads[11].wait()
    arrived("swap", gath.at[1 - core])

    low = iota((8, 8, 128), 2) < 64

    def narrow(k, carry):
        a0 = gath[0, k, :, :, 64:80, :].reshape(16, 16, 128).astype(F32)
        a1 = gath[1, k, :, :, 64:80, :].reshape(16, 16, 128).astype(F32)
        rows = pl.ds(pl.multiple_of(k * 128, 128), 128)
        out_w[rows, 0:128] = a0[:, 0:8].reshape(128, 128).astype(BF)
        out_w[rows, 128:256] = a0[:, 8:16].reshape(128, 128).astype(BF)
        out_w[rows, 256:384] = a1[:, 8:16].reshape(128, 128).astype(BF)
        pairs = a1[:, 0:8].reshape(8, 2, 8, 128)
        te, to = pairs[:, 0], pairs[:, 1]
        t8 = jnp.where(low, te, to)
        b8 = pltpu.roll(jnp.where(low, to, te), 64, 2)
        fold_w[:, pl.ds(pl.multiple_of(k * 1024, 1024), 1024)] = jnp.concatenate(
            [jnp.concatenate([t8[m], b8[m]], axis=0) for m in range(8)], axis=1
        ).astype(BF)
        return carry

    lax.fori_loop(0, NY, narrow, 0)
    right_t = nt(fold_w[...], xs[...])
    mixed = nn(masked[...], out_w[...])
    outward, grad = mixed[:, :256], mixed[:, 256:]

    def wide(h):
        return jnp.concatenate(
            [gath[h, k, :, :, 0:64, :].reshape(1024, 128) for k in range(NY)], axis=0
        )

    w = jnp.concatenate([wide(0), wide(1)], axis=1)
    inward = nn(xs[...], w)

    own = lax.rem(iota((128, 256), 0), 8) == iota((128, 256), 1) // SEQ
    spread_k = one_hot_rows(128, 16, 8)
    rd = nn(spread_k, rk_down[...]).astype(BF)
    left_t = jnp.where(own, nt(rd, grad.astype(BF)), 0.0).astype(BF)
    right_t = jnp.where(own, nn(spread_k, right_t.astype(BF)), 0.0).astype(BF)
    gl = nn(left_t, inward.astype(BF))
    gr = nn(right_t, outward.astype(BF))
    joined = jnp.concatenate(
        [g[8 * k : 8 * k + 8] for g in (gl, gr) for k in range(16)], axis=1
    )
    inv = lax.rsqrt(jnp.sum(joined * joined, axis=1, keepdims=True) / 8192.0 + EPS)
    normed = joined * inv
    feats[...] = normed.astype(BF)

    upper = iota((8, 512), 0) < 4
    for b in range(NY):
        lo = normed[:, 1024 * b : 1024 * b + 512]
        hi = normed[:, 1024 * b + 512 : 1024 * b + 1024]
        f_out[b] = jnp.where(upper, lo, pltpu.roll(hi, 4, 0)).astype(BF)
        p_out[b] = jnp.where(upper, pltpu.roll(lo, 4, 0), hi).astype(BF)
    for d in (4, 3, 5, 2, 6, 1, 7):
        to = lax.rem(y + d, NY)
        send(f_out.at[to], fblk.at[zl, y], at(dy=d), "feature", ("piece", d))
        send(p_out.at[to], pblk.at[x, y], at(dy=d), "feature", ("piece", d))
    fblk[zl, y] = f_out[y]
    pblk[x, y] = p_out[y]

    def pass_on(p):
        f, q = fblk.at[zl, p], pblk.at[x, p]
        for d in (3, 2, 1):
            send(f, f, at(z_in=lax.rem(zl + d, NZ)), "cands", "cands")
        for d in (2, 1, 3):
            send(q, q, at(dx=d), "probes", "probes")

    pass_on(y)
    for d in (1, 7, 2, 6, 3, 5, 4):
        arrived(("piece", d), f_out.at[pl.ds(0, 2)])
        pass_on(ring(y - d, NY))
    arrived("cands", fblk.at[pl.ds(0, 3)])
    arrived("probes", pblk.at[pl.ds(0, 3)])

    def halves(ref):
        lo, hi = [], []
        for k in range(4):
            for m in range(4):
                a, b = ref[k, 2 * m].astype(F32), ref[k, 2 * m + 1].astype(F32)
                lo.append(jnp.where(upper, a, pltpu.roll(b, 4, 0)))
                hi.append(jnp.where(upper, pltpu.roll(a, 4, 0), b))
        return tuple(jnp.concatenate(v, axis=0).astype(BF) for v in (lo, hi))

    f_lo, f_hi = halves(fblk)
    p_lo, p_hi = halves(pblk)
    prod = nt(f_lo, p_lo) + nt(f_hi, p_hi)

    upper = iota((8, 128), 0) < 4
    tile = lambda zq, m: prod[zq * 32 + m * 8 : zq * 32 + m * 8 + 8]
    for m in range(4):
        for h in range(2):
            a, b = tile(2 * h, m), tile(2 * h + 1, m)
            tsum[2 * m, 8 * h : 8 * h + 8] = jnp.where(upper, a, pltpu.roll(b, 4, 0))
            tsum[2 * m + 1, 8 * h : 8 * h + 8] = jnp.where(upper, pltpu.roll(a, 4, 0), b)
    tgot[y] = tsum[y]
    for d in (4, 3, 5, 2, 6, 1, 7):
        send(tsum.at[lax.rem(y + d, NY)], tgot.at[y], at(dy=d), "sums", "sums")
    arrived("sums", tgot.at[pl.ds(0, 7)])
    total = tgot[0]
    for k in range(1, NY):
        total = total + tgot[k]
    vsum[0] = total[0:8]
    vsum[1] = total[8:16]
    vgot[zl] = vsum[zl // 2]
    for d in range(1, NZ):
        tz = lax.rem(zl + d, NZ)
        send(vsum.at[tz // 2], vgot.at[zl], at(z_in=tz), "rows", "rows")
    arrived("rows", vgot.at[pl.ds(0, 3)])
    odd_z = lax.rem(zl, 2) == 1
    flat = jnp.concatenate(
        [jnp.where(odd_z, pltpu.roll(vgot[k], 4, 0), vgot[k]) for k in range(NZ)], axis=1
    )
    p1 = flat.astype(BF).astype(F32)
    p2 = (flat - p1).astype(BF).astype(F32)
    pieces = nn(jnp.concatenate([p1, p2, flat - p1 - p2], axis=0).astype(BF), perm[...])
    out_rows = pieces[0:8] + pieces[8:16] + pieces[16:24]
    scores[...] = out_rows * (1.0 / 8192.0)

    for group, ref in (
        ("a1", gath.at[core, y, zl, pl.ds(0, 3), pl.ds(0, 32)]),
        ("b1", gath.at[core, pl.ds(0, 7), zl, x, pl.ds(32, 48)]),
        ("a2", gath.at[core, y, pl.ds(0, 3), :, pl.ds(0, 32)]),
        ("plane", gath.at[core, pl.ds(0, 4), :, :, pl.ds(0, 32)]),
        ("forward", gath.at[core, pl.ds(0, 3), :, :, pl.ds(0, 32)]),
        ("b2", gath.at[core, pl.ds(0, 6), :, x, pl.ds(32, 48)]),
        ("b3", gath.at[core, pl.ds(0, 6), :, :, pl.ds(32, 48)]),
        ("swap", gath.at[core]),
        ("feature", fblk.at[pl.ds(0, 2), pl.ds(0, 7)]),
        ("cands", fblk.at[pl.ds(0, 3)]),
        ("probes", pblk.at[pl.ds(0, 3)]),
        ("sums", tsum.at[pl.ds(0, 7)]),
        ("rows", vgot.at[pl.ds(0, 3)]),
    ):
        left(group, ref)
    assert len(names["send"]) == N_SEND and len(names["recv"]) == N_RECV, names


def own_rows(scores, feats, own_scores, own_feats):
    own_scores[...] = scores[0:4]
    own_feats[...] = feats[0:4]


def body(xc, ct_c, len_c, xp, ct_p, len_p, down, up, win, wout, rk_down, rk_up):
    width, values = xc.shape[2], ct_c.shape[2]
    anyspace = pl.BlockSpec(memory_space=pl.ANY)
    vmem = pl.BlockSpec(memory_space=pltpu.VMEM)
    scores, feats = pl.pallas_call(
        kernel,
        out_shape=(
            jax.ShapeDtypeStruct((8, 512), F32),
            jax.ShapeDtypeStruct((8, 8192), BF),
        ),
        in_specs=[anyspace] * 12,
        out_specs=(vmem, vmem),
        scratch_shapes=[
            pltpu.SMEM((4,), jnp.int32),
            pltpu.SMEM((4,), jnp.int32),
            pltpu.VMEM((64, 128), BF),
            pltpu.VMEM((8, 128), BF),
            pltpu.VMEM((8, 256), BF),
            pltpu.VMEM((16, 128), BF),
            pltpu.VMEM((16, 128), BF),
            pltpu.VMEM((2, NY, NZ, NX, 80, 128), BF),
            pltpu.VMEM((256, 8192), BF),
            pltpu.VMEM((256, 1024), BF),
            pltpu.VMEM((256, 1024), BF),
            pltpu.VMEM((NY, 8, 512), BF),
            pltpu.VMEM((NY, 8, 512), BF),
            pltpu.VMEM((NZ, NY, 8, 512), BF),
            pltpu.VMEM((NX, NY, 8, 512), BF),
            pltpu.VMEM((NY, 16, 128), F32),
            pltpu.VMEM((NY, 16, 128), F32),
            pltpu.VMEM((2, 8, 128), F32),
            pltpu.VMEM((NZ, 8, 128), F32),
            pltpu.VMEM((512, 512), BF),
            pltpu.VMEM((1024, 384), BF),
            pltpu.VMEM((16, 8192), BF),
            pltpu.SemaphoreType.DMA((12,)),
            pltpu.SemaphoreType.DMA((N_SEND,)),
            pltpu.SemaphoreType.DMA((N_RECV,)),
        ],
        compiler_params=pltpu.CompilerParams(
            collective_id=0, has_side_effects=True, vmem_limit_bytes=67043328
        ),
        name="lora_scores",
    )(
        xc.reshape(-1, width), ct_c.reshape(-1, values), len_c,
        xp.reshape(-1, width), ct_p.reshape(-1, values), len_p,
        down, up, win, wout, rk_down.T, rk_up.T,
    )
    return pl.pallas_call(
        own_rows,
        out_shape=(
            jax.ShapeDtypeStruct((4, 512), F32),
            jax.ShapeDtypeStruct((4, 8192), BF),
        ),
        in_specs=[vmem, vmem],
        out_specs=(vmem, vmem),
        name="own_rows",
    )(scores, feats)


def solution(mesh):
    split = Mesh(mesh.devices.reshape(NY, NZ, NX, 2, 2), AXES)
    rows = P(FSDP, None)
    whole = P(DP_FSDP, None, None)
    return jax.shard_map(
        body,
        mesh=split,
        in_specs=(
            whole, whole, P(DP_FSDP), whole, whole, P(DP_FSDP), rows, rows, rows, rows, P(), P(),
        ),
        out_specs=(P(DP_FSDP, None), P(DP_FSDP, None)),
        check_vma=False,
    )
```

```python
import jax
import jax.numpy as jnp
from jax import lax
from jax.experimental import pallas as pl
from jax.experimental.pallas import tpu as pltpu
from jax.sharding import Mesh
from jax.sharding import PartitionSpec as P

AXES = ("y", "zl", "x", "zh", "core")
FSDP = ("y", "zl", "x")
DP_FSDP = ("zh", "core", "y", "zl", "x")
NY, NZ, NX = 8, 4, 4
SEQ = 32
EPS = 1e-06
BF, F32 = jnp.bfloat16, jnp.float32

N_SEND, N_RECV = 13, 47


def nt(a, b):
    return lax.dot_general(a, b, (((1,), (1,)), ((), ())), preferred_element_type=F32)


def nn(a, b):
    return jnp.dot(a, b, preferred_element_type=F32)


def iota(shape, dim):
    return lax.broadcasted_iota(jnp.int32, shape, dim)


def one_hot_rows(rows, cols, per):
    return (iota((rows, cols), 0) // per == iota((rows, cols), 1)).astype(F32).astype(BF)


def kernel(
    xc, ct_c, len_ch, xp, ct_p, len_ph, down_h, up_h, win_h, wout_h, rk_down_h, rk_up_h,
    scores, feats,
    len_c, len_p, down, up, wout, rk_down, rk_up,
    gath, xs, cot, masked, f_out, p_out, fblk, pblk, tsum, tgot, vsum, vgot, perm, out_w, fold_w, f_rows,
    ld_sem, send_sem, recv_sem,
):
    y, zl, x = (lax.axis_index(a) for a in FSDP)
    zh, core = lax.axis_index("zh"), lax.axis_index("core")
    zz = zh * NZ + zl

    def at(dy=0, dx=0, dz=0, z_in=None, other=False):
        if z_in is None:
            full = lax.rem(zz + dz + 8, 8)
            tz, th = lax.rem(full, NZ), full // NZ
        else:
            tz, th = z_in, zh
        return (
            lax.rem(y + dy + NY, NY),
            tz,
            lax.rem(x + dx + NX, NX),
            th,
            1 - core if other else core,
        )

    loads = [
        pltpu.make_async_copy(src, dst, ld_sem.at[k])
        for k, (src, dst) in enumerate(
            (
                (win_h.at[:, pl.ds(pl.multiple_of(core * 128, 128), 128)], gath.at[core, y, zl, x, pl.ds(0, 64)]),
                (rk_up_h, rk_up),
                (down_h, down),
                (up_h, up),
                (wout_h, wout),
                (rk_down_h, rk_down),
                (len_ch, len_c),
                (len_ph, len_p),
                (ct_c, cot.at[pl.ds(0, 128)]),
                (ct_p, cot.at[pl.ds(128, 128)]),
                (xc, xs.at[pl.ds(0, 128)]),
                (xp, xs.at[pl.ds(128, 128)]),
            )
        )
    ]
    for c in loads:
        c.start()

    barrier = pltpu.get_barrier_semaphore()
    partners = [at(dy=d) for d in range(1, NY)] + [at(dx=d) for d in range(1, NX)]
    partners += [at(z_in=lax.rem(zl + d, NZ)) for d in range(1, NZ)]
    partners += [at(dz=d) for d in (1, -1, 2, -2)] + [at(other=True)]
    for dev in partners:
        pl.semaphore_signal(barrier, inc=1, device_id=dev, device_id_type=pl.DeviceIdType.MESH)

    loads[0].wait()
    pl.semaphore_wait(barrier, len(partners))

    names = {}

    def key(kind, name):
        return names.setdefault(kind, {}).setdefault(name, len(names.get(kind, {})))

    def send(src, dst, dev, group, arrival):
        pltpu.make_async_remote_copy(
            src_ref=src,
            dst_ref=dst,
            send_sem=send_sem.at[key("send", group)],
            recv_sem=recv_sem.at[key("recv", arrival)],
            device_id=dev,
            device_id_type=pl.DeviceIdType.MESH,
        ).start()

    def arrived(arrival, ref):
        pltpu.make_async_copy(ref, ref, recv_sem.at[key("recv", arrival)]).wait()

    def left(group, ref):
        pltpu.make_async_copy(ref, ref, send_sem.at[key("send", group)]).wait()

    def mask_rows():
        loads[8].wait()
        loads[9].wait()
        pos = iota((SEQ, 1024), 0)
        for e in range(8):
            live = (len_c if e < 4 else len_p)[e % 4]
            rows = cot[e * SEQ : (e + 1) * SEQ, :].astype(F32)
            masked[e * SEQ : (e + 1) * SEQ, :] = jnp.where(pos < live, rows, 0.0).astype(BF)

    every = slice(None)
    ring = lambda p, n: lax.rem(p + n, n)

    def rows_a(p, zq, xs=every):
        return gath.at[core, p, zq, xs, pl.ds(0, 32)]

    def rows_b(lo, n, zq, xq):
        return gath.at[core, pl.ds(lo, n), zq, xq, pl.ds(32, 48)]

    def swap(ref):
        send(ref, ref, at(other=True), "swap", "swap")

    def out(ref, group, arrival, **d):
        send(ref, ref, at(**d), group, arrival)

    def a_plane(zq, c):
        ref = rows_a(y, zq)
        swap(ref)
        for d in (2, -2):
            out(ref, "plane", ("two", c, d), dy=d)
        for d in (1, -1):
            out(ref, "plane", ("near", c), dy=d)

    def a_forward(zq, c):
        for sign, lo in ((1, 0), (-1, 2)):
            ref = rows_a(ring(y - 2 * sign, NY), zq)
            arrived(("two", c, 2 * sign), ref)
            out(rows_a(ring(y - 2 * sign, NY), zq, pl.ds(lo, 2)), "forward", ("far", c), dy=2 * sign)
            out(ref, "forward", ("far", c), dy=sign)
            swap(ref)

    def a_near(zq, c):
        arrived(("near", c), gath.at[core, pl.ds(0, 2), zq, :, pl.ds(0, 32)])
        for d in (1, -1):
            swap(rows_a(ring(y + d, NY), zq))

    def a_far(zq, c):
        arrived(("far", c), gath.at[core, pl.ds(0, 3), zq, :, pl.ds(0, 32)])
        for d in (3, -3, 4):
            swap(rows_a(ring(y + d, NY), zq))

    def over_z(lo, zq, xq, group, arrivals):
        ref = rows_b(lo, 4, zq, xq)
        out(ref, group, arrivals[0], dz=1)
        out(ref, group, arrivals[1], dz=-1)
        out(rows_b(lo, 2, zq, xq), group, arrivals[2], dz=2)
        out(rows_b(lo + 2, 2, zq, xq), group, arrivals[2], dz=-2)

    def over_x(lo, zq, xq, group, arrivals):
        ref = rows_b(lo, 4, zq, xq)
        for d, name in zip((2, 1, 3), arrivals):
            out(ref, group, name, dx=d)

    z_from = (ring(zl - 1, NZ), ring(zl + 1, NZ), ring(zl + 2, NZ))
    x_from = (ring(x - 2, NX), ring(x - 1, NX), ring(x - 3, NX))

    own_a = rows_a(y, zl, x)
    own_b = gath.at[core, y, zl, x, pl.ds(32, 32)]
    own_c = gath.at[core, y, zl, x, pl.ds(64, 16)]
    for d in (2, 1, 3):
        out(own_a, "a1", "a1", dx=d)
    for d in (4, 3, 5, 2, 6, 1, 7):
        out(own_b, "b1", "b1", dy=d)
    for c in loads[1:8]:
        c.wait()
    ru = rk_up[...].astype(F32)
    top, bottom = ru[0:8], ru[8:16]
    odd = lax.rem(x, 2) == 1
    one = jnp.where(odd, bottom, top)
    two = jnp.where(odd, top, bottom)
    dn = down[...]
    zero = jnp.zeros_like(dn)
    stacked = jnp.concatenate(
        [jnp.concatenate([dn, zero], axis=1), jnp.concatenate([zero, dn], axis=1)], axis=0
    )
    fold = nt(jnp.concatenate([one, two], axis=1).astype(BF), stacked)
    aux_1 = jnp.concatenate([fold, up[...].astype(F32)], axis=0)
    wo = wout[...].astype(F32)
    aux_0 = jnp.concatenate([wo[:, :128], wo[:, 128:]], axis=0)
    first = core == 0
    gath[core, y, zl, x, 64:80, :] = jnp.where(first, aux_0, aux_1).astype(BF)
    for d in (4, 3, 5, 2, 6, 1, 7):
        out(own_c, "b1", "b1", dy=d)
    mask_rows()
    arrived("a1", gath.at[core, y, zl, pl.ds(0, 3), pl.ds(0, 32)])
    mine = rows_a(y, zl)
    out(mine, "a2", "a2-", dz=1)
    out(mine, "a2", "a2+", dz=-1)
    out(rows_a(y, zl, pl.ds(0, 2)), "a2", "a2=", dz=2)
    out(rows_a(y, zl, pl.ds(2, 2)), "a2", "a2=", dz=-2)
    a_plane(zl, 0)
    src, col = iota((512, 512), 0), iota((512, 512), 1)
    want = ((col >> 4) & 3) * 128 + ((col >> 2) & 3) * 32 + (col >> 6) * 4 + (col & 3)
    perm[...] = (src == want).astype(F32).astype(BF)
    arrived("b1", gath.at[core, pl.ds(0, 7), zl, x, pl.ds(32, 48)])
    over_z(0, zl, x, "b2", ("bx2-", "bx2+", "bx2="))
    over_x(4, zl, x, "b2", ("bz2a", "bz2b", "bz2c"))
    over_x(0, zl, x, "b3", (("bx3", 0),) * 3)
    over_z(4, zl, x, "b3", (("bz3", 0),) * 3)
    swap(rows_b(0, 8, zl, x))
    for c, name in enumerate(("a2-", "a2+", "a2=")):
        arrived(name, rows_a(y, z_from[c]))
        a_plane(z_from[c], c + 1)
    a_forward(zl, 0)
    a_near(zl, 0)

    def bx_next(c, name):
        zq = z_from[c]
        arrived(name, rows_b(0, 4, zq, x))
        over_x(0, zq, x, "b3", (("bx3", c + 1),) * 3)
        swap(rows_b(0, 4, zq, x))

    def bz_next(c, name):
        xq = x_from[c]
        arrived(name, rows_b(4, 4, zl, xq))
        over_z(4, zl, xq, "b3", (("bz3", c + 1),) * 3)
        swap(rows_b(4, 4, zl, xq))

    bx_next(0, "bx2-")
    bz_next(1, "bz2b")
    bx_next(1, "bx2+")
    bz_next(2, "bz2c")
    bz_next(0, "bz2a")
    bx_next(2, "bx2=")
    for c in range(3):
        a_forward(z_from[c], c + 1)
        a_near(z_from[c], c + 1)
    bz_order = (x, x_from[0], x_from[1], x_from[2])
    for c, zq in enumerate((zl,) + z_from):
        arrived(("bx3", c), gath.at[core, pl.ds(0, 4), zq, pl.ds(0, 3), pl.ds(32, 48)])
        for xq in x_from:
            swap(rows_b(0, 4, zq, xq))
        xq = bz_order[c]
        arrived(("bz3", c), gath.at[core, pl.ds(4, 4), pl.ds(0, 3), xq, pl.ds(32, 48)])
        for zr in z_from:
            swap(rows_b(4, 4, zr, xq))
        a_far(zq, c)
    loads[10].wait()
    loads[11].wait()
    arrived("swap", gath.at[1 - core])

    low = iota((8, 8, 128), 2) < 64

    def narrow(k, carry):
        a0 = gath[0, k, :, :, 64:80, :].reshape(16, 16, 128).astype(F32)
        a1 = gath[1, k, :, :, 64:80, :].reshape(16, 16, 128).astype(F32)
        rows = pl.ds(pl.multiple_of(k * 128, 128), 128)
        out_w[rows, 0:128] = a0[:, 0:8].reshape(128, 128).astype(BF)
        out_w[rows, 128:256] = a0[:, 8:16].reshape(128, 128).astype(BF)
        out_w[rows, 256:384] = a1[:, 8:16].reshape(128, 128).astype(BF)
        pairs = a1[:, 0:8].reshape(8, 2, 8, 128)
        te, to = pairs[:, 0], pairs[:, 1]
        t8 = jnp.where(low, te, to)
        b8 = pltpu.roll(jnp.where(low, to, te), 64, 2)
        fold_w[:, pl.ds(pl.multiple_of(k * 1024, 1024), 1024)] = jnp.concatenate(
            [jnp.concatenate([t8[m], b8[m]], axis=0) for m in range(8)], axis=1
        ).astype(BF)
        return carry

    lax.fori_loop(0, NY, narrow, 0)
    right_t = nt(fold_w[...], xs[...])
    mixed = nn(masked[...], out_w[...])
    outward, grad = mixed[:, :256], mixed[:, 256:]

    def wide(h):
        return jnp.concatenate(
            [gath[h, k, :, :, 0:64, :].reshape(1024, 128) for k in range(NY)], axis=0
        )

    w = jnp.concatenate([wide(0), wide(1)], axis=1)
    inward = nn(xs[...], w)

    own = lax.rem(iota((128, 256), 0), 8) == iota((128, 256), 1) // SEQ
    spread_k = one_hot_rows(128, 16, 8)
    rd = nn(spread_k, rk_down[...]).astype(BF)
    left_t = jnp.where(own, nt(rd, grad.astype(BF)), 0.0).astype(BF)
    right_t = jnp.where(own, nn(spread_k, right_t.astype(BF)), 0.0).astype(BF)
    gl = nn(left_t, inward.astype(BF))
    gr = nn(right_t, outward.astype(BF))
    joined = jnp.concatenate(
        [g[8 * k : 8 * k + 8] for g in (gl, gr) for k in range(16)], axis=1
    )
    inv = lax.rsqrt(jnp.sum(joined * joined, axis=1, keepdims=True) / 8192.0 + EPS)
    normed = joined * inv
    f_rows[...] = normed.astype(BF)
    store = pltpu.make_async_copy(f_rows, feats, ld_sem.at[12])
    store.start()

    upper = iota((8, 512), 0) < 4
    for b in range(NY):
        lo = normed[:, 1024 * b : 1024 * b + 512]
        hi = normed[:, 1024 * b + 512 : 1024 * b + 1024]
        f_out[b] = jnp.where(upper, lo, pltpu.roll(hi, 4, 0)).astype(BF)
        p_out[b] = jnp.where(upper, pltpu.roll(lo, 4, 0), hi).astype(BF)
    for d in (4, 3, 5, 2, 6, 1, 7):
        to = lax.rem(y + d, NY)
        send(f_out.at[to], fblk.at[zl, y], at(dy=d), "feature", ("piece", d))
        send(p_out.at[to], pblk.at[x, y], at(dy=d), "feature", ("piece", d))
    fblk[zl, y] = f_out[y]
    pblk[x, y] = p_out[y]

    def pass_on(p):
        f, q = fblk.at[zl, p], pblk.at[x, p]
        for d in (3, 2, 1):
            send(f, f, at(z_in=lax.rem(zl + d, NZ)), "cands", "cands")
        for d in (2, 1, 3):
            send(q, q, at(dx=d), "probes", "probes")

    pass_on(y)
    for d in (1, 7, 2, 6, 3, 5, 4):
        arrived(("piece", d), f_out.at[pl.ds(0, 2)])
        pass_on(ring(y - d, NY))
    arrived("cands", fblk.at[pl.ds(0, 3)])
    arrived("probes", pblk.at[pl.ds(0, 3)])

    def halves(ref):
        lo, hi = [], []
        for k in range(4):
            for m in range(4):
                a, b = ref[k, 2 * m].astype(F32), ref[k, 2 * m + 1].astype(F32)
                lo.append(jnp.where(upper, a, pltpu.roll(b, 4, 0)))
                hi.append(jnp.where(upper, pltpu.roll(a, 4, 0), b))
        return tuple(jnp.concatenate(v, axis=0).astype(BF) for v in (lo, hi))

    f_lo, f_hi = halves(fblk)
    p_lo, p_hi = halves(pblk)
    prod = nt(f_lo, p_lo) + nt(f_hi, p_hi)

    upper = iota((8, 128), 0) < 4
    tile = lambda zq, m: prod[zq * 32 + m * 8 : zq * 32 + m * 8 + 8]
    for m in range(4):
        for h in range(2):
            a, b = tile(2 * h, m), tile(2 * h + 1, m)
            tsum[2 * m, 8 * h : 8 * h + 8] = jnp.where(upper, a, pltpu.roll(b, 4, 0))
            tsum[2 * m + 1, 8 * h : 8 * h + 8] = jnp.where(upper, pltpu.roll(a, 4, 0), b)
    tgot[y] = tsum[y]
    for d in (4, 3, 5, 2, 6, 1, 7):
        send(tsum.at[lax.rem(y + d, NY)], tgot.at[y], at(dy=d), "sums", "sums")
    arrived("sums", tgot.at[pl.ds(0, 7)])
    total = tgot[0]
    for k in range(1, NY):
        total = total + tgot[k]
    vsum[0] = total[0:8]
    vsum[1] = total[8:16]
    vgot[zl] = vsum[zl // 2]
    for d in range(1, NZ):
        tz = lax.rem(zl + d, NZ)
        send(vsum.at[tz // 2], vgot.at[zl], at(z_in=tz), "rows", "rows")
    arrived("rows", vgot.at[pl.ds(0, 3)])
    odd_z = lax.rem(zl, 2) == 1
    flat = jnp.concatenate(
        [jnp.where(odd_z, pltpu.roll(vgot[k], 4, 0), vgot[k]) for k in range(NZ)], axis=1
    )
    p1 = flat.astype(BF).astype(F32)
    p2 = (flat - p1).astype(BF).astype(F32)
    pieces = nn(jnp.concatenate([p1, p2, flat - p1 - p2], axis=0).astype(BF), perm[...])
    out_rows = pieces[0:8] + pieces[8:16] + pieces[16:24]
    scores[...] = out_rows * (1.0 / 8192.0)

    store.wait()
    for group, ref in (
        ("a1", gath.at[core, y, zl, pl.ds(0, 3), pl.ds(0, 32)]),
        ("b1", gath.at[core, pl.ds(0, 7), zl, x, pl.ds(32, 48)]),
        ("a2", gath.at[core, y, pl.ds(0, 3), :, pl.ds(0, 32)]),
        ("plane", gath.at[core, pl.ds(0, 4), :, :, pl.ds(0, 32)]),
        ("forward", gath.at[core, pl.ds(0, 3), :, :, pl.ds(0, 32)]),
        ("b2", gath.at[core, pl.ds(0, 6), :, x, pl.ds(32, 48)]),
        ("b3", gath.at[core, pl.ds(0, 6), :, :, pl.ds(32, 48)]),
        ("swap", gath.at[core]),
        ("feature", fblk.at[pl.ds(0, 2), pl.ds(0, 7)]),
        ("cands", fblk.at[pl.ds(0, 3)]),
        ("probes", pblk.at[pl.ds(0, 3)]),
        ("sums", tsum.at[pl.ds(0, 7)]),
        ("rows", vgot.at[pl.ds(0, 3)]),
    ):
        left(group, ref)
    assert len(names["send"]) == N_SEND and len(names["recv"]) == N_RECV, names


def own_rows(scores, feats, own_scores, own_feats):
    own_scores[...] = scores[0:4]
    own_feats[...] = feats[0:4]


def body(xc, ct_c, len_c, xp, ct_p, len_p, down, up, win, wout, rk_down, rk_up):
    width, values = xc.shape[2], ct_c.shape[2]
    anyspace = pl.BlockSpec(memory_space=pl.ANY)
    vmem = pl.BlockSpec(memory_space=pltpu.VMEM)
    scores, feats = pl.pallas_call(
        kernel,
        out_shape=(
            jax.ShapeDtypeStruct((8, 512), F32),
            jax.ShapeDtypeStruct((8, 8192), BF),
        ),
        in_specs=[anyspace] * 12,
        out_specs=(vmem, anyspace),
        scratch_shapes=[
            pltpu.SMEM((4,), jnp.int32),
            pltpu.SMEM((4,), jnp.int32),
            pltpu.VMEM((64, 128), BF),
            pltpu.VMEM((8, 128), BF),
            pltpu.VMEM((8, 256), BF),
            pltpu.VMEM((16, 128), BF),
            pltpu.VMEM((16, 128), BF),
            pltpu.VMEM((2, NY, NZ, NX, 80, 128), BF),
            pltpu.VMEM((256, 8192), BF),
            pltpu.VMEM((256, 1024), BF),
            pltpu.VMEM((256, 1024), BF),
            pltpu.VMEM((NY, 8, 512), BF),
            pltpu.VMEM((NY, 8, 512), BF),
            pltpu.VMEM((NZ, NY, 8, 512), BF),
            pltpu.VMEM((NX, NY, 8, 512), BF),
            pltpu.VMEM((NY, 16, 128), F32),
            pltpu.VMEM((NY, 16, 128), F32),
            pltpu.VMEM((2, 8, 128), F32),
            pltpu.VMEM((NZ, 8, 128), F32),
            pltpu.VMEM((512, 512), BF),
            pltpu.VMEM((1024, 384), BF),
            pltpu.VMEM((16, 8192), BF),
            pltpu.VMEM((8, 8192), BF),
            pltpu.SemaphoreType.DMA((13,)),
            pltpu.SemaphoreType.DMA((N_SEND,)),
            pltpu.SemaphoreType.DMA((N_RECV,)),
        ],
        compiler_params=pltpu.CompilerParams(
            collective_id=0, has_side_effects=True, vmem_limit_bytes=67043328
        ),
        name="lora_scores",
    )(
        xc.reshape(-1, width), ct_c.reshape(-1, values), len_c,
        xp.reshape(-1, width), ct_p.reshape(-1, values), len_p,
        down, up, win, wout, rk_down.T, rk_up.T,
    )
    return pl.pallas_call(
        own_rows,
        out_shape=(
            jax.ShapeDtypeStruct((4, 512), F32),
            jax.ShapeDtypeStruct((4, 8192), BF),
        ),
        in_specs=[vmem, vmem],
        out_specs=(vmem, vmem),
        name="own_rows",
    )(scores, feats)


def solution(mesh):
    split = Mesh(mesh.devices.reshape(NY, NZ, NX, 2, 2), AXES)
    rows = P(FSDP, None)
    whole = P(DP_FSDP, None, None)
    return jax.shard_map(
        body,
        mesh=split,
        in_specs=(
            whole, whole, P(DP_FSDP), whole, whole, P(DP_FSDP), rows, rows, rows, rows, P(), P(),
        ),
        out_specs=(P(DP_FSDP, None), P(DP_FSDP, None)),
        check_vma=False,
    )
```
